128 devices in a mesh: dp: 8 (over z_hi, x), shard: 16 (over y, z_lo, core).
Axes of the slice: x: 4, y: 4, z: 4 (z_hi: 2, z_lo: 2; z = z_hi * 2 + z_lo), core: 2. Of those that a mesh axis runs over, the one named last changes fastest.
Arguments:
- gradients: bfloat16 [8, 8, 1572864], P('dp', None, 'shard'), may hold values from -32 to 32
- master: float32 [12582912], P(('dp', 'shard'))
- moment: float32 [12582912], P(('dp', 'shard')), may hold values from -1.5 to 1.5
- second: float32 [12582912], P(('dp', 'shard')), may hold values from 0.05 to 2
- segment_ids: int32 [98304], P(('dp', 'shard')), may hold values from 0 to 63, never falling along the last dimension, each value on 1 to 3072 neighbouring positions
Outputs:
- weights: bfloat16 [8, 1572864], P(None, 'shard')
- new_master: float32 [12582912], P(('dp', 'shard'))
- new_moment: float32 [12582912], P(('dp', 'shard'))
- new_second: float32 [12582912], P(('dp', 'shard'))
The draws below stay inside these ranges and needn't reach their ends.
Inputs may be any that keep to these rules, and one draw needn't show every extreme that they name: segment_ids never falls along the flat vector; each tensor has 1 to 3072 blocks and one has exactly 3072.
All inputs are finite; a program needn't handle non-finite values.
Results may differ from the reference program's by a relative error of at most 0.0004.
Values may be sent and summed in bfloat16 or wider, within the bound.
A program may use at most 64 MiB of HBM per device.

```python
import math
import jax
import jax.numpy as jnp
import numpy as np
from jax import lax

BLOCK = 128
LOCAL_BLOCKS = 768
FLAT = 12582912
TENSORS = 64
MOST = 3072
N_DP = 8
DEVICES = 128


def draw_master(key, part):
    noise_key = jax.random.fold_in(key, 11)
    scale_key = jax.random.fold_in(key, 12)
    range_key = jax.random.fold_in(key, 13)
    position = jnp.arange(FLAT, dtype=jnp.float32) / FLAT
    rising = jnp.exp(jnp.log(3.0) * position)
    block_scale = jax.random.uniform(scale_key, (FLAT // BLOCK,), jnp.float32, 0.5, 2.0)
    block_scale = jnp.repeat(block_scale, BLOCK)
    ranges = FLAT // (BLOCK * LOCAL_BLOCKS)
    range_log = jax.random.uniform(range_key, (ranges,), jnp.float32, 0.0, jnp.log(10.0))
    range_scale = jnp.repeat(jnp.exp(range_log), BLOCK * LOCAL_BLOCKS)
    values = jax.random.normal(noise_key, (FLAT,), jnp.float32)
    values = values * rising * block_scale * range_scale
    return values.astype(jnp.float32)


def raised(array, rng, source, target, parts, factor):
    def block_of(dim):
        return (jnp.arange(array.shape[dim]) // (array.shape[dim] // parts)).reshape((-1,) + (1,) * (array.ndim - 1 - dim))

    near = jax.random.permutation(rng, parts)[block_of(target)]
    far = (block_of(target) + parts // 2) % parts
    return jnp.where((block_of(source) == near) | (block_of(source) == far), factor * array, array)


def shard_levels(rng, dims, cuts, least, top_value):
    level, own = 1.0, jax.random.fold_in(rng, 6)
    for axis_at, parts in cuts:
        draws = jnp.exp(jax.random.uniform(jax.random.fold_in(own, axis_at), (parts,), jnp.float32, least / len(cuts), top_value / len(cuts)))
        level = level * jnp.repeat(draws, dims[axis_at] // parts).reshape([-1 if axis == axis_at else 1 for axis in range(len(dims))])
    return level


def split_up(count, total, bound, slope):
    portions = [(1 << 20) // math.isqrt(rank ** slope) + 1 for rank in range(2, count + 1)]
    surplus, counts = total - bound - (count - 1), [1] * (count - 1)
    while surplus > 0:
        free = [i for i in range(count - 1) if counts[i] < bound]
        whole, remaining = sum([portions[i] for i in free]), surplus
        for i in free:
            addition = min(bound - counts[i], max(1, remaining * portions[i] // whole), surplus)
            counts[i] = counts[i] + addition
            surplus = surplus - addition
    return np.array([bound] + counts)


def uneven(stream_key, number_of, total, bound, lean):
    if number_of == 2:
        one = jax.random.randint(stream_key, (), max(1, total - bound), min(bound, total - 1) + 1)
        return jnp.stack([one, total - one])
    lengths = jnp.asarray(split_up(number_of, total, bound, lean), jnp.int32)
    couples = (number_of - 1) // 2
    source_of, taker = lengths[1:1 + 2 * couples:2], lengths[2:2 + 2 * couples:2]
    margin = jnp.minimum(source_of - 1, bound - taker)
    moved = jax.random.randint(jax.random.fold_in(stream_key, 1), (couples,), 0, 1 << 20) % (margin + 1)
    lengths = lengths.at[1:1 + 2 * couples:2].set(source_of - moved).at[2:2 + 2 * couples:2].set(taker + moved)
    return lengths[jax.random.permutation(jax.random.fold_in(stream_key, 2), number_of)]


def normal_values(rng, extent, width, limit, pieces=(), kind=jnp.bfloat16):
    drawn = width * jax.random.normal(rng, extent, jnp.float32)
    if pieces:
        drawn = drawn * shard_levels(rng, extent, pieces, -0.22, 0.18)
    return jnp.clip(drawn, -limit, limit).astype(kind)


def gaussian_with(stream_key, dims, spread, limit, pieces, heavy, kind=jnp.bfloat16):
    result = spread * jax.random.normal(stream_key, dims, jnp.float32)
    if pieces:
        result = result * shard_levels(stream_key, dims, pieces, -0.22, 0.18)
    return jnp.clip(raised(result, jax.random.fold_in(stream_key, 3), *heavy), -limit, limit).astype(kind)


def setup_inputs(seed: int = 0) -> dict:
    key_list = jax.random.split(jax.random.key(seed), 6)
    gradients = gaussian_with(key_list[0], (N_DP, N_DP, FLAT // N_DP), 4.0, 32.0, ((0, 8), (2, 16)), (0, 1, 8, 2.0))
    master = draw_master(jax.random.fold_in(key_list[5], 71), 0)
    moment = normal_values(key_list[2], (FLAT,), 0.1, 1.5, ((0, 128),), jnp.float32)
    second = jnp.clip(jnp.exp(math.log(2.0) - 3.6888794 * jax.random.uniform(key_list[3], (FLAT,), jnp.float32) ** shard_levels(key_list[3], (FLAT,), ((0, 128),), -0.2, 0.2)), 0.05, 2.0)
    segment_ids = jnp.searchsorted(jnp.cumsum(uneven(key_list[4], TENSORS, LOCAL_BLOCKS * DEVICES, MOST, 2)), jnp.arange(LOCAL_BLOCKS * DEVICES), side="right").astype(jnp.int32)
    return {"gradients": gradients, "master": master, "moment": moment, "second": second, "segment_ids": segment_ids}


first_fix = 1.0 - 0.9 ** 20
second_fix = 1.0 - 0.999 ** 20
learn_rate = 0.2
decay_rate = 0.01
tiny_eps = 1e-06

def reference(gradients, master, moment, second, segment_ids):
    grad = lax.optimization_barrier(jnp.sum(gradients.astype(jnp.float32), axis=0)).reshape(-1) / N_DP
    new_moment = 0.9 * moment + 0.1 * grad
    new_second = 0.999 * second + 0.001 * grad * grad
    update = new_moment / first_fix / (jnp.sqrt(new_second / second_fix) + tiny_eps) + decay_rate * master
    weight_blocks = lax.optimization_barrier(jnp.sum((master * master).reshape(-1, BLOCK), axis=1))
    update_blocks = lax.optimization_barrier(jnp.sum((update * update).reshape(-1, BLOCK), axis=1))
    weight_sq = jax.ops.segment_sum(weight_blocks, segment_ids, num_segments=TENSORS)
    update_sq = jax.ops.segment_sum(update_blocks, segment_ids, num_segments=TENSORS)
    trust = jnp.sqrt(weight_sq) / (jnp.sqrt(update_sq) + tiny_eps)
    block_trust = trust[segment_ids]
    new_master = master - learn_rate * (update.reshape(-1, BLOCK) * block_trust[:, None]).reshape(-1)
    weights = new_master.astype(jnp.bfloat16).reshape(N_DP, -1)
    return (weights, new_master, new_moment, new_second)
```

```python
import functools

import jax
import jax.numpy as jnp
from jax import lax
from jax.experimental import pallas as pl
from jax.experimental.pallas import tpu as pltpu
from jax.sharding import Mesh
from jax.sharding import PartitionSpec as P

AXES = ("zh", "x", "y", "zl", "core")
DP = ("zh", "x")
SHARD = ("y", "zl", "core")
DP_SHARD = AXES
MESH = pl.DeviceIdType.MESH

first_fix = 1.0 - 0.9**20
second_fix = 1.0 - 0.999**20
learn_rate = 0.2
decay_rate = 0.01
tiny_eps = 1e-06

REPLICAS = 8
TENSORS = 64
BLOCKS = 768
LANES = 128
CHUNK = 128
CHUNKS = BLOCKS // CHUNK
SUB = 32
PIECE = 64
PIECES = BLOCKS // PIECE
REACH = 4
LAG = 4
HIGH = lax.Precision.HIGHEST

STEPS = ((1, 0), (3, 0), (0, 1), (2, 1), (2, 0), (1, 1), (3, 1))
X_STEPS = (1, 3, 2)
OFFSETS = tuple(range(-REACH, 0)) + tuple(range(1, REACH + 1))


def place():
    return {axis: lax.axis_index(axis) for axis in AXES}


def replica_at(here, x_step, z_step):
    there = dict(here)
    there["x"] = lax.rem(here["x"] + x_step, 4)
    there["zh"] = lax.rem(here["zh"] + z_step, 2)
    return there


def row_of(there):
    return there["zh"] * 4 + there["x"]


def flat_neighbour(here, offset):
    rank = (((here["zh"] * 4 + here["x"]) * 4 + here["y"]) * 2 + here["zl"]) * 2 + here["core"]
    rank = lax.rem(rank + offset + 128, 128)
    return {
        "zh": rank // 64,
        "x": lax.rem(rank // 16, 4),
        "y": lax.rem(rank // 4, 4),
        "zl": lax.rem(rank // 2, 2),
        "core": lax.rem(rank, 2),
    }


def remote(src, dst, send_sem, recv_sem, there):
    return pltpu.make_async_remote_copy(
        src_ref=src,
        dst_ref=dst,
        send_sem=send_sem,
        recv_sem=recv_sem,
        device_id=there,
        device_id_type=MESH,
    )


def kernel(
    grad_hbm, master_hbm, moment_hbm, second_hbm, ids_hbm,
    weights_out, master_out, moment_out, second_out,
    grad_in, rows, got, master, moment, second, update, ids, squares, sums,
    mine, theirs, spread, gathered, packed,
    load_sem, state_sem, send_sem, recv_sem, sum_send, sum_recv,
    out_send, out_recv, store_sem, state_out_sem,
):
    here = place()
    me = row_of(here)
    peers = [replica_at(here, a, b) for a, b in STEPS]
    neighbours = [flat_neighbour(here, k) for k in OFFSETS]

    def load(c):
        cols = pl.ds(pl.multiple_of(c * CHUNK * LANES, CHUNK * LANES), CHUNK * LANES)
        return pltpu.make_async_copy(grad_hbm.at[:, cols], grad_in.at[:, cols], load_sem.at[c])

    for c in range(CHUNKS):
        load(c).start()
    state_loads = [
        pltpu.make_async_copy(src, dst, state_sem.at[i])
        for i, (src, dst) in enumerate(
            ((ids_hbm, ids), (master_hbm, master), (moment_hbm, moment), (second_hbm, second))
        )
    ]
    for copy in state_loads:
        copy.start()

    barrier = pltpu.get_barrier_semaphore()
    for there in peers + neighbours:
        pl.semaphore_signal(barrier, inc=1, device_id=there, device_id_type=MESH)

    def split_rows(c):
        load(c).wait()

        def tile(t, carry):
            at = c * CHUNK + t * 8
            for i in range(8):
                cols = pl.ds(pl.multiple_of((at + i) * LANES, LANES), LANES)
                spread[pl.ds(pl.multiple_of((t * 8 + i) * 8, 8), 8), :] = grad_in[:, cols].astype(
                    jnp.float32
                )
            return carry

        lax.fori_loop(0, CHUNK // 8, tile, 0)
        for r in range(REPLICAS):
            for h in range(CHUNK // SUB):
                piece = spread[pl.ds(h * SUB * 8 + r, SUB, stride=8), :]
                rows[r, pl.ds(pl.multiple_of(c * CHUNK + h * SUB, SUB), SUB), :] = piece.astype(
                    jnp.bfloat16
                )

    def exchange(c, k):
        part = pl.ds(pl.multiple_of(c * CHUNK, CHUNK), CHUNK)
        return remote(
            rows.at[row_of(peers[k]), part], got.at[k, part],
            send_sem.at[c, k], recv_sem.at[c, k], peers[k],
        )

    def send_chunk(c, carry):
        split_rows(c)

        @pl.when(c == 0)
        def _():
            pl.semaphore_wait(barrier, len(peers) + len(neighbours))

        for k in range(len(STEPS)):
            exchange(c, k).start()
        return carry

    lax.fori_loop(0, CHUNKS, send_chunk, 0)

    for copy in state_loads:
        copy.wait()

    def onehot(c):
        tensor = lax.broadcasted_iota(jnp.int32, (TENSORS, CHUNK), 0)
        return (tensor == ids[pl.ds(c, 1), :]).astype(jnp.float32)

    sums[...] = jnp.zeros_like(sums)

    def weigh(c, carry):
        values = master[pl.ds(pl.multiple_of(c * CHUNK, CHUNK), CHUNK), :]
        sums[:TENSORS, :] += jnp.dot(
            onehot(c), values * values, precision=HIGH, preferred_element_type=jnp.float32
        )
        return carry

    lax.fori_loop(0, CHUNKS, weigh, 0)

    def step_chunk(c, carry):
        for k in range(len(STEPS)):
            exchange(c, k).wait_recv()
        for h in range(CHUNK // SUB):
            part = pl.ds(pl.multiple_of(c * CHUNK + h * SUB, SUB), SUB)
            total = rows[me, part, :].astype(jnp.float32)
            for k in range(len(STEPS)):
                total = total + got[k, part, :].astype(jnp.float32)
            grad = total / REPLICAS
            next_moment = 0.9 * moment[part, :] + 0.1 * grad
            next_second = 0.999 * second[part, :] + 0.001 * grad * grad
            change = (
                next_moment / first_fix / (jnp.sqrt(next_second / second_fix) + tiny_eps)
                + decay_rate * master[part, :]
            )
            moment[part, :] = next_moment
            second[part, :] = next_second
            update[part, :] = change
            squares[pl.ds(h * SUB, SUB), :] = change * change
        sums[TENSORS:, :] += jnp.dot(
            onehot(c), squares[...], precision=HIGH, preferred_element_type=jnp.float32
        )
        return carry

    lax.fori_loop(0, CHUNKS, step_chunk, 0)

    ones = jnp.ones((8, LANES), jnp.float32)
    mine[...] = lax.dot_general(
        ones, sums[...], (((1,), (1,)), ((), ())), precision=HIGH,
        preferred_element_type=jnp.float32,
    )
    swaps = [
        remote(mine, theirs.at[i], sum_send.at[i], sum_recv.at[i], neighbours[len(OFFSETS) - 1 - i])
        for i in range(len(OFFSETS))
    ]
    for copy in swaps:
        copy.start()
    state_stores = [
        pltpu.make_async_copy(moment, moment_out, state_out_sem.at[0]),
        pltpu.make_async_copy(second, second_out, state_out_sem.at[1]),
    ]
    for copy in state_stores:
        copy.start()
    for copy in swaps:
        copy.wait_recv()
    total = mine[...]
    for i in range(len(OFFSETS)):
        total = total + theirs[i]
    trust = jnp.sqrt(total) / (jnp.sqrt(pltpu.roll(total, TENSORS, 1)) + tiny_eps)
    trust_row = trust[:1, :]
    diagonal = lax.broadcasted_iota(jnp.int32, (TENSORS, LANES), 0) == lax.broadcasted_iota(
        jnp.int32, (TENSORS, LANES), 1
    )
    trust_of = jnp.sum(jnp.where(diagonal, trust_row, 0.0), axis=1, keepdims=True)
    trust_of = jnp.broadcast_to(trust_of, (TENSORS, LANES))

    partner = replica_at(here, 0, 1)
    beside = [replica_at(here, a, 0) for a in X_STEPS]
    behind = [replica_at(here, 4 - a, 0) for a in X_STEPS]
    direct_to = [partner] + beside
    direct_from = [partner] + behind
    far_from = [replica_at(here, 4 - a, 1) for a in X_STEPS]

    def piece_of(p):
        return pl.ds(pl.multiple_of(p * PIECE, PIECE), PIECE)

    def direct(p, i):
        block = gathered.at[me, piece_of(p)]
        return remote(block, block, out_send.at[p, i], out_recv.at[p, i], direct_to[i])

    def arrived(p, i, source):
        block = gathered.at[row_of(source), piece_of(p)]
        return remote(block, block, out_send.at[p, i], out_recv.at[p, i], partner)

    def onward_x(p, j):
        block = gathered.at[row_of(partner), piece_of(p)]
        return remote(block, block, out_send.at[p, 4 + j], out_recv.at[p, 4 + j], beside[j])

    def onward_z(p, j):
        block = gathered.at[row_of(behind[j]), piece_of(p)]
        return remote(block, block, out_send.at[p, 4 + j], out_recv.at[p, 4 + j], partner)

    def finish_chunk(c, carry):
        trust_block = lax.dot_general(
            onehot(c), trust_of, (((0,), (0,)), ((), ())), precision=HIGH,
            preferred_element_type=jnp.float32,
        )
        part = pl.ds(pl.multiple_of(c * CHUNK, CHUNK), CHUNK)
        new_master = master[part, :] - learn_rate * (update[part, :] * trust_block)
        master[part, :] = new_master
        gathered[me, part, :] = new_master.astype(jnp.bfloat16)
        for half in range(CHUNK // PIECE):
            for i in range(4):
                direct(c * (CHUNK // PIECE) + half, i).start()
        return carry

    lax.fori_loop(0, CHUNKS, finish_chunk, 0)
    state_stores.append(pltpu.make_async_copy(master, master_out, state_out_sem.at[2]))
    state_stores[2].start()

    def z_first(p):
        return lax.rem(p * 5, 12) < 5

    def forward(p):
        @pl.when(z_first(p))
        def _():
            arrived(p, 0, partner).wait_recv()
            for j in range(3):
                onward_x(p, j).start()

        @pl.when(jnp.logical_not(z_first(p)))
        def _():
            for j in range(3):
                arrived(p, 1 + j, behind[j]).wait_recv()
                onward_z(p, j).start()

    def store(p):
        cols = pl.ds(pl.multiple_of(p * PIECE * LANES, PIECE * LANES), PIECE * LANES)
        return pltpu.make_async_copy(packed.at[:, cols], weights_out.at[:, cols], store_sem.at[p])

    def collect(p):
        @pl.when(z_first(p))
        def _():
            for j in range(3):
                arrived(p, 1 + j, behind[j]).wait_recv()

        @pl.when(jnp.logical_not(z_first(p)))
        def _():
            arrived(p, 0, partner).wait_recv()

        for j in range(3):
            arrived(p, 4 + j, far_from[j]).wait_recv()
        for r in range(REPLICAS):
            spread[pl.ds(r, PIECE, stride=8), :] = gathered[r, piece_of(p), :].astype(jnp.float32)

        def tile(t, carry):
            for i in range(8):
                at = t * 8 + i
                cols = pl.ds(pl.multiple_of((p * PIECE + at) * LANES, LANES), LANES)
                packed[:, cols] = spread[pl.ds(pl.multiple_of(at * 8, 8), 8), :].astype(
                    jnp.bfloat16
                )
            return carry

        lax.fori_loop(0, PIECE // 8, tile, 0)
        store(p).start()

    def gather_step(s, carry):
        @pl.when(s < PIECES)
        def _():
            forward(s)

        @pl.when(s >= LAG)
        def _():
            collect(s - LAG)

        return carry

    lax.fori_loop(0, PIECES + LAG, gather_step, 0)

    def drain(c, carry):
        for k in range(len(STEPS)):
            exchange(c, k).wait_send()
        return carry

    lax.fori_loop(0, CHUNKS, drain, 0)

    def drain_out(p, carry):
        for i in range(7):
            remote(
                gathered.at[me, piece_of(p)], gathered.at[me, piece_of(p)],
                out_send.at[p, i], out_recv.at[p, i], partner,
            ).wait_send()
        store(p).wait()
        return carry

    lax.fori_loop(0, PIECES, drain_out, 0)
    for copy in swaps:
        copy.wait_send()
    for copy in state_stores:
        copy.wait()


def on_device(gradients, master, moment, second, segment_ids):
    flat = master.shape[0]
    tall = (BLOCKS, LANES)
    f32, bf16 = jnp.float32, jnp.bfloat16
    any_spec = pl.BlockSpec(memory_space=pl.ANY)
    dma = pltpu.SemaphoreType.DMA
    weights, new_master, new_moment, new_second = pl.pallas_call(
        kernel,
        out_shape=(
            jax.ShapeDtypeStruct((REPLICAS, flat), bf16),
            jax.ShapeDtypeStruct(tall, f32),
            jax.ShapeDtypeStruct(tall, f32),
            jax.ShapeDtypeStruct(tall, f32),
        ),
        in_specs=[pl.BlockSpec(memory_space=pltpu.HBM)] * 5,
        out_specs=(any_spec,) * 4,
        scratch_shapes=[
            pltpu.VMEM((REPLICAS, flat), bf16),
            pltpu.VMEM((REPLICAS, BLOCKS, LANES), bf16),
            pltpu.VMEM((len(STEPS), BLOCKS, LANES), bf16),
            pltpu.VMEM(tall, f32),
            pltpu.VMEM(tall, f32),
            pltpu.VMEM(tall, f32),
            pltpu.VMEM(tall, f32),
            pltpu.VMEM((CHUNKS, CHUNK), jnp.int32),
            pltpu.VMEM((CHUNK, LANES), f32),
            pltpu.VMEM((2 * TENSORS, LANES), f32),
            pltpu.VMEM((8, LANES), f32),
            pltpu.VMEM((len(OFFSETS), 8, LANES), f32),
            pltpu.VMEM((CHUNK * 8, LANES), f32),
            pltpu.VMEM((REPLICAS, BLOCKS, LANES), bf16),
            pltpu.VMEM((REPLICAS, flat), bf16),
            dma((CHUNKS,)),
            dma((4,)),
            dma((CHUNKS, len(STEPS))),
            dma((CHUNKS, len(STEPS))),
            dma((len(OFFSETS),)),
            dma((len(OFFSETS),)),
            dma((PIECES, 7)),
            dma((PIECES, 7)),
            dma((PIECES,)),
            dma((3,)),
        ],
        compiler_params=pltpu.CompilerParams(
            collective_id=0, has_side_effects=True, vmem_limit_bytes=40 << 20
        ),
        name="lamb_step",
    )(
        gradients.reshape(REPLICAS, flat),
        master.reshape(tall),
        moment.reshape(tall),
        second.reshape(tall),
        segment_ids.reshape(CHUNKS, CHUNK),
    )
    return (weights, new_master.reshape(-1), new_moment.reshape(-1), new_second.reshape(-1))


def solution(mesh):
    torus = Mesh(mesh.devices.reshape(2, 4, 4, 2, 2), AXES)
    return jax.shard_map(
        on_device,
        mesh=torus,
        in_specs=(P(DP, None, SHARD), P(DP_SHARD), P(DP_SHARD), P(DP_SHARD), P(DP_SHARD)),
        out_specs=(P(None, SHARD), P(DP_SHARD), P(DP_SHARD), P(DP_SHARD)),
        check_vma=False,
    )
```

```python
import functools

import jax
import jax.numpy as jnp
from jax import lax
from jax.experimental import pallas as pl
from jax.experimental.pallas import tpu as pltpu
from jax.sharding import Mesh
from jax.sharding import PartitionSpec as P

AXES = ("zh", "x", "y", "zl", "core")
DP = ("zh", "x")
SHARD = ("y", "zl", "core")
DP_SHARD = AXES
MESH = pl.DeviceIdType.MESH

first_fix = 1.0 - 0.9**20
second_fix = 1.0 - 0.999**20
learn_rate = 0.2
decay_rate = 0.01
tiny_eps = 1e-06

REPLICAS = 8
TENSORS = 64
BLOCKS = 768
LANES = 128
CHUNK = 128
CHUNKS = BLOCKS // CHUNK
SUB = 32
PIECE = 64
PIECES = BLOCKS // PIECE
REACH = 4
Z_FIRST = (0, 2, 4, 6, 8, 10)
X_FIRST = tuple(p for p in range(PIECES) if p not in Z_FIRST)
HIGH = lax.Precision.HIGHEST

STEPS = ((1, 1), (3, 0), (2, 1), (1, 0), (0, 1), (3, 1), (2, 0))
X_STEPS = (1, 3, 2)
OFFSETS = tuple(range(-REACH, 0)) + tuple(range(1, REACH + 1))


def place():
    return {axis: lax.axis_index(axis) for axis in AXES}


def replica_at(here, x_step, z_step):
    there = dict(here)
    there["x"] = lax.rem(here["x"] + x_step, 4)
    there["zh"] = lax.rem(here["zh"] + z_step, 2)
    return there


def row_of(there):
    return there["zh"] * 4 + there["x"]


def flat_neighbour(here, offset):
    rank = (((here["zh"] * 4 + here["x"]) * 4 + here["y"]) * 2 + here["zl"]) * 2 + here["core"]
    rank = lax.rem(rank + offset + 128, 128)
    return {
        "zh": rank // 64,
        "x": lax.rem(rank // 16, 4),
        "y": lax.rem(rank // 4, 4),
        "zl": lax.rem(rank // 2, 2),
        "core": lax.rem(rank, 2),
    }


def remote(src, dst, send_sem, recv_sem, there):
    return pltpu.make_async_remote_copy(
        src_ref=src,
        dst_ref=dst,
        send_sem=send_sem,
        recv_sem=recv_sem,
        device_id=there,
        device_id_type=MESH,
    )


def kernel(
    grad_hbm, master_hbm, moment_hbm, second_hbm, ids_hbm,
    packed, master, moment, second,
    grad_in, rows, got, update, ids, squares, sums,
    mine, theirs, spread, gathered,
    load_sem, state_sem, send_sem, recv_sem, sum_send, sum_recv,
    out_send, out_recv,
):
    here = place()
    me = row_of(here)
    peers = [replica_at(here, a, b) for a, b in STEPS]
    neighbours = [flat_neighbour(here, k) for k in OFFSETS]

    def load(c):
        cols = pl.ds(pl.multiple_of(c * CHUNK * LANES, CHUNK * LANES), CHUNK * LANES)
        return pltpu.make_async_copy(grad_hbm.at[:, cols], grad_in.at[:, cols], load_sem.at[c])

    for c in range(CHUNKS):
        load(c).start()
    state_loads = [
        pltpu.make_async_copy(src, dst, state_sem.at[i])
        for i, (src, dst) in enumerate(
            ((ids_hbm, ids), (master_hbm, master), (moment_hbm, moment), (second_hbm, second))
        )
    ]
    for copy in state_loads:
        copy.start()

    barrier = pltpu.get_barrier_semaphore()
    for there in peers + neighbours:
        pl.semaphore_signal(barrier, inc=1, device_id=there, device_id_type=MESH)

    def split_rows(c):
        load(c).wait()

        def tile(t, carry):
            at = c * CHUNK + t * 8
            for i in range(8):
                cols = pl.ds(pl.multiple_of((at + i) * LANES, LANES), LANES)
                spread[pl.ds(pl.multiple_of((t * 8 + i) * 8, 8), 8), :] = grad_in[:, cols].astype(
                    jnp.float32
                )
            return carry

        lax.fori_loop(0, CHUNK // 8, tile, 0)
        for r in range(REPLICAS):
            for h in range(CHUNK // SUB):
                piece = spread[pl.ds(h * SUB * 8 + r, SUB, stride=8), :]
                rows[r, pl.ds(pl.multiple_of(c * CHUNK + h * SUB, SUB), SUB), :] = piece.astype(
                    jnp.bfloat16
                )

    def exchange(c, k):
        part = pl.ds(pl.multiple_of(c * CHUNK, CHUNK), CHUNK)
        return remote(
            rows.at[row_of(peers[k]), part], got.at[k, part],
            send_sem.at[c, k], recv_sem.at[c, k], peers[k],
        )

    def send_chunk(c, carry):
        split_rows(c)

        @pl.when(c == 0)
        def _():
            pl.semaphore_wait(barrier, len(peers) + len(neighbours))

        for k in range(len(STEPS)):
            exchange(c, k).start()
        return carry

    lax.fori_loop(0, CHUNKS, send_chunk, 0)

    for copy in state_loads:
        copy.wait()

    def onehot(c):
        tensor = lax.broadcasted_iota(jnp.int32, (TENSORS, CHUNK), 0)
        return (tensor == ids[pl.ds(c, 1), :]).astype(jnp.float32)

    sums[...] = jnp.zeros_like(sums)

    def weigh(c, carry):
        values = master[pl.ds(pl.multiple_of(c * CHUNK, CHUNK), CHUNK), :]
        sums[:TENSORS, :] += jnp.dot(
            onehot(c), values * values, precision=HIGH, preferred_element_type=jnp.float32
        )
        return carry

    lax.fori_loop(0, CHUNKS, weigh, 0)

    def step_chunk(c, carry):
        for k in range(len(STEPS)):
            exchange(c, k).wait_recv()
        for h in range(CHUNK // SUB):
            part = pl.ds(pl.multiple_of(c * CHUNK + h * SUB, SUB), SUB)
            total = rows[me, part, :].astype(jnp.float32)
            for k in range(len(STEPS)):
                total = total + got[k, part, :].astype(jnp.float32)
            grad = total / REPLICAS
            next_moment = 0.9 * moment[part, :] + 0.1 * grad
            next_second = 0.999 * second[part, :] + 0.001 * grad * grad
            change = (
                next_moment / first_fix / (jnp.sqrt(next_second / second_fix) + tiny_eps)
                + decay_rate * master[part, :]
            )
            moment[part, :] = next_moment
            second[part, :] = next_second
            update[part, :] = change
            squares[pl.ds(h * SUB, SUB), :] = change * change
        sums[TENSORS:, :] += jnp.dot(
            onehot(c), squares[...], precision=HIGH, preferred_element_type=jnp.float32
        )
        return carry

    lax.fori_loop(0, CHUNKS, step_chunk, 0)

    ones = jnp.ones((8, LANES), jnp.float32)
    mine[...] = lax.dot_general(
        ones, sums[...], (((1,), (1,)), ((), ())), precision=HIGH,
        preferred_element_type=jnp.float32,
    )
    swaps = [
        remote(mine, theirs.at[i], sum_send.at[i], sum_recv.at[i], neighbours[len(OFFSETS) - 1 - i])
        for i in range(len(OFFSETS))
    ]
    for copy in swaps:
        copy.start()
    for copy in swaps:
        copy.wait_recv()
    total = mine[...]
    for i in range(len(OFFSETS)):
        total = total + theirs[i]
    trust = jnp.sqrt(total) / (jnp.sqrt(pltpu.roll(total, TENSORS, 1)) + tiny_eps)
    trust_row = trust[:1, :]
    diagonal = lax.broadcasted_iota(jnp.int32, (TENSORS, LANES), 0) == lax.broadcasted_iota(
        jnp.int32, (TENSORS, LANES), 1
    )
    trust_of = jnp.sum(jnp.where(diagonal, trust_row, 0.0), axis=1, keepdims=True)
    trust_of = jnp.broadcast_to(trust_of, (TENSORS, LANES))

    partner = replica_at(here, 0, 1)
    beside = [replica_at(here, a, 0) for a in X_STEPS]
    behind = [replica_at(here, 4 - a, 0) for a in X_STEPS]
    direct_to = [partner] + beside
    direct_from = [partner] + behind
    far_from = [replica_at(here, 4 - a, 1) for a in X_STEPS]

    def piece_of(p):
        return pl.ds(pl.multiple_of(p * PIECE, PIECE), PIECE)

    def direct(p, i):
        block = gathered.at[me, piece_of(p)]
        return remote(block, block, out_send.at[p, i], out_recv.at[p, i], direct_to[i])

    def arrived(p, i, source):
        block = gathered.at[row_of(source), piece_of(p)]
        return remote(block, block, out_send.at[p, i], out_recv.at[p, i], partner)

    def onward_x(p, j):
        block = gathered.at[row_of(partner), piece_of(p)]
        return remote(block, block, out_send.at[p, 4 + j], out_recv.at[p, 4 + j], beside[j])

    def onward_z(p, j):
        block = gathered.at[row_of(behind[j]), piece_of(p)]
        return remote(block, block, out_send.at[p, 4 + j], out_recv.at[p, 4 + j], partner)

    def finish_chunk(c):
        trust_block = lax.dot_general(
            onehot(c), trust_of, (((0,), (0,)), ((), ())), precision=HIGH,
            preferred_element_type=jnp.float32,
        )
        part = pl.ds(c * CHUNK, CHUNK)
        new_master = master[part, :] - learn_rate * (update[part, :] * trust_block)
        master[part, :] = new_master
        gathered[me, part, :] = new_master.astype(jnp.bfloat16)

    def forward_x(p):
        arrived(p, 0, partner).wait_recv()
        for j in range(3):
            onward_x(p, j).start()

    def forward_z(p):
        for j in range(3):
            arrived(p, 1 + j, behind[j]).wait_recv()
            onward_z(p, j).start()

    def collect(p):
        if p in Z_FIRST:
            for j in range(3):
                arrived(p, 1 + j, behind[j]).wait_recv()
        else:
            arrived(p, 0, partner).wait_recv()
        for j in range(3):
            arrived(p, 4 + j, far_from[j]).wait_recv()
        for r in range(REPLICAS):
            spread[pl.ds(r, PIECE, stride=8), :] = gathered[r, piece_of(p), :].astype(jnp.float32)

        def tile(t, carry):
            for i in range(8):
                at = t * 8 + i
                cols = pl.ds(pl.multiple_of((p * PIECE + at) * LANES, LANES), LANES)
                packed[:, cols] = spread[pl.ds(pl.multiple_of(at * 8, 8), 8), :].astype(
                    jnp.bfloat16
                )
            return carry

        lax.fori_loop(0, PIECE // 8, tile, 0)

    for c in range(CHUNKS):
        finish_chunk(c)
        for p in range(c * PIECES // CHUNKS, (c + 1) * PIECES // CHUNKS):
            if p in Z_FIRST:
                direct(p, 0).start()
            else:
                for i in range(1, 4):
                    direct(p, i).start()
    for p in X_FIRST:
        direct(p, 0).start()
    for k in range(max(len(Z_FIRST), len(X_FIRST))):
        if k < len(Z_FIRST):
            for i in range(1, 4):
                direct(Z_FIRST[k], i).start()
        if k < len(X_FIRST):
            forward_z(X_FIRST[k])
        if k < len(Z_FIRST):
            forward_x(Z_FIRST[k])
    for p in X_FIRST + Z_FIRST:
        collect(p)

    def drain(c, carry):
        for k in range(len(STEPS)):
            exchange(c, k).wait_send()
        return carry

    lax.fori_loop(0, CHUNKS, drain, 0)

    def drain_out(p, carry):
        for i in range(7):
            remote(
                gathered.at[me, piece_of(p)], gathered.at[me, piece_of(p)],
                out_send.at[p, i], out_recv.at[p, i], partner,
            ).wait_send()
        return carry

    lax.fori_loop(0, PIECES, drain_out, 0)
    for copy in swaps:
        copy.wait_send()


def hand_over(*refs):
    sem = refs[-1]
    copies = [pltpu.make_async_copy(refs[i], refs[4 + i], sem.at[i]) for i in range(4)]
    for copy in copies:
        copy.start()
    for copy in copies:
        copy.wait()


def on_device(gradients, master, moment, second, segment_ids):
    flat = master.shape[0]
    tall = (BLOCKS, LANES)
    f32, bf16 = jnp.float32, jnp.bfloat16
    vmem_spec = pl.BlockSpec(memory_space=pltpu.VMEM)
    dma = pltpu.SemaphoreType.DMA
    weights, new_master, new_moment, new_second = pl.pallas_call(
        kernel,
        out_shape=(
            jax.ShapeDtypeStruct((REPLICAS, flat), bf16),
            jax.ShapeDtypeStruct(tall, f32),
            jax.ShapeDtypeStruct(tall, f32),
            jax.ShapeDtypeStruct(tall, f32),
        ),
        in_specs=[pl.BlockSpec(memory_space=pltpu.HBM)] * 5,
        out_specs=(vmem_spec,) * 4,
        scratch_shapes=[
            pltpu.VMEM((REPLICAS, flat), bf16),
            pltpu.VMEM((REPLICAS, BLOCKS, LANES), bf16),
            pltpu.VMEM((len(STEPS), BLOCKS, LANES), bf16),
            pltpu.VMEM(tall, f32),
            pltpu.VMEM((CHUNKS, CHUNK), jnp.int32),
            pltpu.VMEM((CHUNK, LANES), f32),
            pltpu.VMEM((2 * TENSORS, LANES), f32),
            pltpu.VMEM((8, LANES), f32),
            pltpu.VMEM((len(OFFSETS), 8, LANES), f32),
            pltpu.VMEM((CHUNK * 8, LANES), f32),
            pltpu.VMEM((REPLICAS, BLOCKS, LANES), bf16),
            dma((CHUNKS,)),
            dma((4,)),
            dma((CHUNKS, len(STEPS))),
            dma((CHUNKS, len(STEPS))),
            dma((len(OFFSETS),)),
            dma((len(OFFSETS),)),
            dma((PIECES, 7)),
            dma((PIECES, 7)),
        ],
        compiler_params=pltpu.CompilerParams(
            collective_id=0, has_side_effects=True, vmem_limit_bytes=40 << 20
        ),
        name="lamb_step",
    )(
        *(
            pltpu.with_memory_space_constraint(array, pltpu.HBM)
            for array in (
                gradients.reshape(REPLICAS, flat),
                master.reshape(tall),
                moment.reshape(tall),
                second.reshape(tall),
                segment_ids.reshape(CHUNKS, CHUNK),
            )
        )
    )
    weights, new_master, new_moment, new_second = pl.pallas_call(
        hand_over,
        out_shape=(
            jax.ShapeDtypeStruct((REPLICAS, flat), bf16),
            jax.ShapeDtypeStruct(tall, f32),
            jax.ShapeDtypeStruct(tall, f32),
            jax.ShapeDtypeStruct(tall, f32),
        ),
        in_specs=[vmem_spec] * 4,
        out_specs=(pl.BlockSpec(memory_space=pltpu.HBM),) * 4,
        scratch_shapes=[dma((4,))],
        compiler_params=pltpu.CompilerParams(vmem_limit_bytes=8 << 20),
        name="hand_over",
    )(weights, new_master, new_moment, new_second)
    return (weights, new_master.reshape(-1), new_moment.reshape(-1), new_second.reshape(-1))


def solution(mesh):
    torus = Mesh(mesh.devices.reshape(2, 4, 4, 2, 2), AXES)
    return jax.shard_map(
        on_device,
        mesh=torus,
        in_specs=(P(DP, None, SHARD), P(DP_SHARD), P(DP_SHARD), P(DP_SHARD), P(DP_SHARD)),
        out_specs=(P(None, SHARD), P(DP_SHARD), P(DP_SHARD), P(DP_SHARD)),
        check_vma=False,
    )
```

```python
import functools

import jax
import jax.numpy as jnp
from jax import lax
from jax.experimental import pallas as pl
from jax.experimental.pallas import tpu as pltpu
from jax.sharding import Mesh
from jax.sharding import PartitionSpec as P

AXES = ("zh", "x", "y", "zl", "core")
DP = ("zh", "x")
SHARD = ("y", "zl", "core")
DP_SHARD = AXES
MESH = pl.DeviceIdType.MESH

first_fix = 1.0 - 0.9**20
second_fix = 1.0 - 0.999**20
learn_rate = 0.2
decay_rate = 0.01
tiny_eps = 1e-06

REPLICAS = 8
TENSORS = 64
BLOCKS = 768
LANES = 128
CHUNK = 128
CHUNKS = BLOCKS // CHUNK
SUB = 32
PIECE = 64
PIECES = BLOCKS // PIECE
REACH = 4
Z_FIRST = (0, 2, 4, 6, 8, 10)
X_FIRST = tuple(p for p in range(PIECES) if p not in Z_FIRST)
HIGH = lax.Precision.HIGHEST

STEPS = ((1, 1), (3, 0), (2, 1), (1, 0), (0, 1), (3, 1), (2, 0))
X_STEPS = (1, 3, 2)
OFFSETS = tuple(range(-REACH, 0)) + tuple(range(1, REACH + 1))


def place():
    return {axis: lax.axis_index(axis) for axis in AXES}


def replica_at(here, x_step, z_step):
    there = dict(here)
    there["x"] = lax.rem(here["x"] + x_step, 4)
    there["zh"] = lax.rem(here["zh"] + z_step, 2)
    return there


def row_of(there):
    return there["zh"] * 4 + there["x"]


def flat_neighbour(here, offset):
    rank = (((here["zh"] * 4 + here["x"]) * 4 + here["y"]) * 2 + here["zl"]) * 2 + here["core"]
    rank = lax.rem(rank + offset + 128, 128)
    return {
        "zh": rank // 64,
        "x": lax.rem(rank // 16, 4),
        "y": lax.rem(rank // 4, 4),
        "zl": lax.rem(rank // 2, 2),
        "core": lax.rem(rank, 2),
    }


def remote(src, dst, send_sem, recv_sem, there):
    return pltpu.make_async_remote_copy(
        src_ref=src,
        dst_ref=dst,
        send_sem=send_sem,
        recv_sem=recv_sem,
        device_id=there,
        device_id_type=MESH,
    )


def kernel(
    grad_hbm, master_hbm, moment_hbm, second_hbm, ids_hbm,
    packed, master, moment, second,
    grad_in, rows, got, update, ids, squares, sums,
    mine, theirs, spread, gathered,
    load_sem, state_sem, send_sem, recv_sem, sum_send, sum_recv,
    out_send, out_recv,
):
    here = place()
    me = row_of(here)
    peers = [replica_at(here, a, b) for a, b in STEPS]
    neighbours = [flat_neighbour(here, k) for k in OFFSETS]

    barrier = pltpu.get_barrier_semaphore()
    for there in peers + neighbours:
        pl.semaphore_signal(barrier, inc=1, device_id=there, device_id_type=MESH)

    def load(c):
        cols = pl.ds(pl.multiple_of(c * CHUNK * LANES, CHUNK * LANES), CHUNK * LANES)
        return pltpu.make_async_copy(grad_hbm.at[:, cols], grad_in.at[:, cols], load_sem.at[c])

    for c in range(CHUNKS):
        load(c).start()
    state_loads = [
        pltpu.make_async_copy(src, dst, state_sem.at[i])
        for i, (src, dst) in enumerate(
            ((ids_hbm, ids), (master_hbm, master), (moment_hbm, moment), (second_hbm, second))
        )
    ]
    for copy in state_loads:
        copy.start()

    def split_rows(c):
        load(c).wait()

        def tile(t, carry):
            at = c * CHUNK + t * 8
            for i in range(8):
                cols = pl.ds(pl.multiple_of((at + i) * LANES, LANES), LANES)
                spread[pl.ds(pl.multiple_of((t * 8 + i) * 8, 8), 8), :] = grad_in[:, cols].astype(
                    jnp.float32
                )
            return carry

        lax.fori_loop(0, CHUNK // 8, tile, 0)
        for r in range(REPLICAS):
            for h in range(CHUNK // SUB):
                piece = spread[pl.ds(h * SUB * 8 + r, SUB, stride=8), :]
                rows[r, pl.ds(pl.multiple_of(c * CHUNK + h * SUB, SUB), SUB), :] = piece.astype(
                    jnp.bfloat16
                )

    def exchange(c, k):
        part = pl.ds(pl.multiple_of(c * CHUNK, CHUNK), CHUNK)
        return remote(
            rows.at[row_of(peers[k]), part], got.at[k, part],
            send_sem, recv_sem.at[c], peers[k],
        )

    def await_chunk(c):
        part = got.at[:, pl.ds(pl.multiple_of(c * CHUNK, CHUNK), CHUNK)]
        remote(part, part, send_sem, recv_sem.at[c], peers[0]).wait_recv()

    def send_chunk(c, carry):
        split_rows(c)

        @pl.when(c == 0)
        def _():
            pl.semaphore_wait(barrier, len(peers) + len(neighbours))

        for k in range(len(STEPS)):
            exchange(c, k).start()
        return carry

    lax.fori_loop(0, CHUNKS, send_chunk, 0)

    for copy in state_loads:
        copy.wait()

    def onehot(c):
        tensor = lax.broadcasted_iota(jnp.int32, (TENSORS, CHUNK), 0)
        return (tensor == ids[pl.ds(c, 1), :]).astype(jnp.float32)

    sums[...] = jnp.zeros_like(sums)

    def weigh(c, carry):
        values = master[pl.ds(pl.multiple_of(c * CHUNK, CHUNK), CHUNK), :]
        sums[:TENSORS, :] += jnp.dot(
            onehot(c), values * values, precision=HIGH, preferred_element_type=jnp.float32
        )
        return carry

    lax.fori_loop(0, CHUNKS, weigh, 0)

    def step_chunk(c, carry):
        await_chunk(c)
        for h in range(CHUNK // SUB):
            part = pl.ds(pl.multiple_of(c * CHUNK + h * SUB, SUB), SUB)
            total = rows[me, part, :].astype(jnp.float32)
            for k in range(len(STEPS)):
                total = total + got[k, part, :].astype(jnp.float32)
            grad = total / REPLICAS
            next_moment = 0.9 * moment[part, :] + 0.1 * grad
            next_second = 0.999 * second[part, :] + 0.001 * grad * grad
            change = (
                next_moment / first_fix / (jnp.sqrt(next_second / second_fix) + tiny_eps)
                + decay_rate * master[part, :]
            )
            moment[part, :] = next_moment
            second[part, :] = next_second
            update[part, :] = change
            squares[pl.ds(h * SUB, SUB), :] = change * change
        sums[TENSORS:, :] += jnp.dot(
            onehot(c), squares[...], precision=HIGH, preferred_element_type=jnp.float32
        )
        return carry

    lax.fori_loop(0, CHUNKS, step_chunk, 0)

    ones = jnp.ones((8, LANES), jnp.float32)
    mine[...] = lax.dot_general(
        ones, sums[...], (((1,), (1,)), ((), ())), precision=HIGH,
        preferred_element_type=jnp.float32,
    )
    swaps = [
        remote(mine, theirs.at[i], sum_send, sum_recv, neighbours[len(OFFSETS) - 1 - i])
        for i in range(len(OFFSETS))
    ]
    for copy in swaps:
        copy.start()
    all_swaps = remote(theirs, theirs, sum_send, sum_recv, neighbours[0])
    all_swaps.wait_recv()
    total = mine[...]
    for i in range(len(OFFSETS)):
        total = total + theirs[i]
    trust = jnp.sqrt(total) / (jnp.sqrt(pltpu.roll(total, TENSORS, 1)) + tiny_eps)
    trust_row = trust[:1, :]
    diagonal = lax.broadcasted_iota(jnp.int32, (TENSORS, LANES), 0) == lax.broadcasted_iota(
        jnp.int32, (TENSORS, LANES), 1
    )
    trust_of = jnp.sum(jnp.where(diagonal, trust_row, 0.0), axis=1, keepdims=True)
    trust_of = jnp.broadcast_to(trust_of, (TENSORS, LANES))

    partner = replica_at(here, 0, 1)
    beside = [replica_at(here, a, 0) for a in X_STEPS]
    behind = [replica_at(here, 4 - a, 0) for a in X_STEPS]
    direct_to = [partner] + beside

    def piece_of(p):
        return pl.ds(pl.multiple_of(p * PIECE, PIECE), PIECE)

    def direct(p, i):
        block = gathered.at[me, piece_of(p)]
        if p in Z_FIRST:
            sem = 0 if i == 0 else 1
        else:
            sem = (2, 0, 0, 1)[i]
        return remote(block, block, out_send, out_recv.at[3 * p + sem], direct_to[i])

    def onward_x(p, j):
        block = gathered.at[row_of(partner), piece_of(p)]
        return remote(block, block, out_send, out_recv.at[3 * p + 1], beside[j])

    def onward_z(p, j):
        block = gathered.at[row_of(behind[j]), piece_of(p)]
        return remote(block, block, out_send, out_recv.at[3 * p + 2], partner)

    def await_pieces(p, sem, count):
        blocks = got.at[pl.ds(0, count), piece_of(p)]
        remote(blocks, blocks, out_send, out_recv.at[3 * p + sem], partner).wait_recv()

    def finish_chunk(c):
        trust_block = lax.dot_general(
            onehot(c), trust_of, (((0,), (0,)), ((), ())), precision=HIGH,
            preferred_element_type=jnp.float32,
        )
        part = pl.ds(c * CHUNK, CHUNK)
        new_master = master[part, :] - learn_rate * (update[part, :] * trust_block)
        master[part, :] = new_master
        gathered[me, part, :] = new_master.astype(jnp.bfloat16)

    def forward_x(p):
        await_pieces(p, 0, 1)
        for j in range(3):
            onward_x(p, j).start()

    def forward_z(p):
        await_pieces(p, 0, 2)
        onward_z(p, 0).start()
        onward_z(p, 1).start()
        await_pieces(p, 1, 1)
        onward_z(p, 2).start()

    def collect(p):
        if p in Z_FIRST:
            await_pieces(p, 1, 6)
        else:
            await_pieces(p, 2, 4)
        for r in range(REPLICAS):
            spread[pl.ds(r, PIECE, stride=8), :] = gathered[r, piece_of(p), :].astype(jnp.float32)

        def tile(t, carry):
            for i in range(8):
                at = t * 8 + i
                cols = pl.ds(pl.multiple_of((p * PIECE + at) * LANES, LANES), LANES)
                packed[:, cols] = spread[pl.ds(pl.multiple_of(at * 8, 8), 8), :].astype(
                    jnp.bfloat16
                )
            return carry

        lax.fori_loop(0, PIECE // 8, tile, 0)

    for c in range(CHUNKS):
        finish_chunk(c)
        for p in range(c * PIECES // CHUNKS, (c + 1) * PIECES // CHUNKS):
            if p in Z_FIRST:
                direct(p, 0).start()
            else:
                for i in range(1, 4):
                    direct(p, i).start()
    for p in X_FIRST:
        direct(p, 0).start()
    for k in range(max(len(Z_FIRST), len(X_FIRST))):
        if k < len(Z_FIRST):
            for i in range(1, 4):
                direct(Z_FIRST[k], i).start()
        if k < len(X_FIRST):
            forward_z(X_FIRST[k])
        if k < len(Z_FIRST):
            forward_x(Z_FIRST[k])
    for p in X_FIRST + Z_FIRST:
        collect(p)

    remote(got, got, send_sem, recv_sem.at[0], partner).wait_send()
    remote(theirs, theirs, sum_send, sum_recv, partner).wait_send()
    remote(got, got, out_send, out_recv.at[0], partner).wait_send()


def hand_over(*refs):
    sem = refs[-1]
    copies = [pltpu.make_async_copy(refs[i], refs[4 + i], sem.at[i]) for i in range(4)]
    for copy in copies:
        copy.start()
    for copy in copies:
        copy.wait()


def on_device(gradients, master, moment, second, segment_ids):
    flat = master.shape[0]
    tall = (BLOCKS, LANES)
    f32, bf16 = jnp.float32, jnp.bfloat16
    vmem_spec = pl.BlockSpec(memory_space=pltpu.VMEM)
    dma = pltpu.SemaphoreType.DMA
    weights, new_master, new_moment, new_second = pl.pallas_call(
        kernel,
        out_shape=(
            jax.ShapeDtypeStruct((REPLICAS, flat), bf16),
            jax.ShapeDtypeStruct(tall, f32),
            jax.ShapeDtypeStruct(tall, f32),
            jax.ShapeDtypeStruct(tall, f32),
        ),
        in_specs=[pl.BlockSpec(memory_space=pltpu.HBM)] * 5,
        out_specs=(vmem_spec,) * 4,
        scratch_shapes=[
            pltpu.VMEM((REPLICAS, flat), bf16),
            pltpu.VMEM((REPLICAS, BLOCKS, LANES), bf16),
            pltpu.VMEM((len(STEPS), BLOCKS, LANES), bf16),
            pltpu.VMEM(tall, f32),
            pltpu.VMEM((CHUNKS, CHUNK), jnp.int32),
            pltpu.VMEM((CHUNK, LANES), f32),
            pltpu.VMEM((2 * TENSORS, LANES), f32),
            pltpu.VMEM((8, LANES), f32),
            pltpu.VMEM((len(OFFSETS), 8, LANES), f32),
            pltpu.VMEM((CHUNK * 8, LANES), f32),
            pltpu.VMEM((REPLICAS, BLOCKS, LANES), bf16),
            dma((CHUNKS,)),
            dma((4,)),
            dma,
            dma((CHUNKS,)),
            dma,
            dma,
            dma,
            dma((PIECES * 3,)),
        ],
        compiler_params=pltpu.CompilerParams(
            collective_id=0, has_side_effects=True, vmem_limit_bytes=40 << 20
        ),
        name="lamb_step",
    )(
        *(
            pltpu.with_memory_space_constraint(array, pltpu.HBM)
            for array in (
                gradients.reshape(REPLICAS, flat),
                master.reshape(tall),
                moment.reshape(tall),
                second.reshape(tall),
                segment_ids.reshape(CHUNKS, CHUNK),
            )
        )
    )
    weights, new_master, new_moment, new_second = pl.pallas_call(
        hand_over,
        out_shape=(
            jax.ShapeDtypeStruct((REPLICAS, flat), bf16),
            jax.ShapeDtypeStruct(tall, f32),
            jax.ShapeDtypeStruct(tall, f32),
            jax.ShapeDtypeStruct(tall, f32),
        ),
        in_specs=[vmem_spec] * 4,
        out_specs=(pl.BlockSpec(memory_space=pltpu.HBM),) * 4,
        scratch_shapes=[dma((4,))],
        compiler_params=pltpu.CompilerParams(vmem_limit_bytes=8 << 20),
        name="hand_over",
    )(weights, new_master, new_moment, new_second)
    return (weights, new_master.reshape(-1), new_moment.reshape(-1), new_second.reshape(-1))


def solution(mesh):
    torus = Mesh(mesh.devices.reshape(2, 4, 4, 2, 2), AXES)
    return jax.shard_map(
        on_device,
        mesh=torus,
        in_specs=(P(DP, None, SHARD), P(DP_SHARD), P(DP_SHARD), P(DP_SHARD), P(DP_SHARD)),
        out_specs=(P(None, SHARD), P(DP_SHARD), P(DP_SHARD), P(DP_SHARD)),
        check_vma=False,
    )
```

```python
import functools

import jax
import jax.numpy as jnp
from jax import lax
from jax.experimental import pallas as pl
from jax.experimental.pallas import tpu as pltpu
from jax.sharding import Mesh
from jax.sharding import PartitionSpec as P

AXES = ("zh", "x", "y", "zl", "core")
DP = ("zh", "x")
SHARD = ("y", "zl", "core")
DP_SHARD = AXES
MESH = pl.DeviceIdType.MESH

first_fix = 1.0 - 0.9**20
second_fix = 1.0 - 0.999**20
learn_rate = 0.2
decay_rate = 0.01
tiny_eps = 1e-06

REPLICAS = 8
TENSORS = 64
BLOCKS = 768
LANES = 128
CHUNK = 128
CHUNKS = BLOCKS // CHUNK
SUB = 32
PIECE = 64
PIECES = BLOCKS // PIECE
REACH = 4
Z_FIRST = (0, 2, 4, 6, 8, 10)
X_FIRST = tuple(p for p in range(PIECES) if p not in Z_FIRST)
LAG = 3
HIGH = lax.Precision.HIGHEST

STEPS = ((1, 1), (3, 0), (2, 1), (1, 0), (0, 1), (3, 1), (2, 0))
X_STEPS = (1, 3, 2)
ROUTES = ("plane", "plane", 1, 3, "direct", "direct")
SUMMED = tuple(c for c in range(CHUNKS) if ROUTES[c] != "direct")
OFFSETS = tuple(range(-REACH, 0)) + tuple(range(1, REACH + 1))


def place():
    return {axis: lax.axis_index(axis) for axis in AXES}


def replica_at(here, x_step, z_step):
    there = dict(here)
    there["x"] = lax.rem(here["x"] + x_step, 4)
    there["zh"] = lax.rem(here["zh"] + z_step, 2)
    return there


def row_of(there):
    return there["zh"] * 4 + there["x"]


def flat_neighbour(here, offset):
    rank = (((here["zh"] * 4 + here["x"]) * 4 + here["y"]) * 2 + here["zl"]) * 2 + here["core"]
    rank = lax.rem(rank + offset + 128, 128)
    return {
        "zh": rank // 64,
        "x": lax.rem(rank // 16, 4),
        "y": lax.rem(rank // 4, 4),
        "zl": lax.rem(rank // 2, 2),
        "core": lax.rem(rank, 2),
    }


def remote(src, dst, send_sem, recv_sem, there):
    return pltpu.make_async_remote_copy(
        src_ref=src,
        dst_ref=dst,
        send_sem=send_sem,
        recv_sem=recv_sem,
        device_id=there,
        device_id_type=MESH,
    )


def kernel(
    grad_hbm, master_hbm, moment_hbm, second_hbm, ids_hbm,
    packed, master, moment, second,
    grad_in, rows, got, sum_out, sum_in, update, ids, picks, squares, sums,
    mine, theirs, spread, gathered,
    load_sem, state_sem, send_sem, recv_sem, sum_send, sum_recv,
    out_send, out_recv,
):
    here = place()
    me = row_of(here)
    peers = [replica_at(here, a, b) for a, b in STEPS]
    neighbours = [flat_neighbour(here, k) for k in OFFSETS]

    barrier = pltpu.get_barrier_semaphore()
    for there in peers + neighbours:
        pl.semaphore_signal(barrier, inc=1, device_id=there, device_id_type=MESH)

    def load(c):
        cols = pl.ds(pl.multiple_of(c * CHUNK * LANES, CHUNK * LANES), CHUNK * LANES)
        return pltpu.make_async_copy(grad_hbm.at[:, cols], grad_in.at[:, cols], load_sem.at[c])

    for c in range(CHUNKS):
        load(c).start()
    state_loads = [
        pltpu.make_async_copy(src, dst, state_sem.at[i])
        for i, (src, dst) in enumerate(
            ((ids_hbm, ids), (master_hbm, master), (moment_hbm, moment), (second_hbm, second))
        )
    ]
    for copy in state_loads:
        copy.start()

    def split_rows(c):
        load(c).wait()

        def tile(t, carry):
            at = c * CHUNK + t * 8
            for i in range(8):
                cols = pl.ds(pl.multiple_of((at + i) * LANES, LANES), LANES)
                spread[pl.ds(pl.multiple_of((t * 8 + i) * 8, 8), 8), :] = grad_in[:, cols].astype(
                    jnp.float32
                )
            return carry

        lax.fori_loop(0, CHUNK // 8, tile, 0)
        for r in range(REPLICAS):
            for h in range(CHUNK // SUB):
                piece = spread[pl.ds(h * SUB * 8 + r, SUB, stride=8), :]
                rows[r, pl.ds(pl.multiple_of(c * CHUNK + h * SUB, SUB), SUB), :] = piece.astype(
                    jnp.bfloat16
                )

    def part_of(c):
        return pl.ds(c * CHUNK, CHUNK)

    partner = replica_at(here, 0, 1)

    def sends(c):
        route = ROUTES[c]
        if route == "direct":
            return [(there, there, k) for k, there in enumerate(peers)]
        if route == "plane":
            out = []
            for j, a in enumerate(X_STEPS):
                there = replica_at(here, a, 0)
                out.append((replica_at(here, a, 1), there, 3 + j))
                out.append((there, there, j))
            return out
        near, back = route, 4 - route
        return [
            (replica_at(here, 2, 1), replica_at(here, back, 1), 4),
            (replica_at(here, 2, 0), replica_at(here, back, 0), 3),
            (replica_at(here, back, 1), partner, 5),
            (replica_at(here, near, 1), replica_at(here, near, 1), 1),
            (partner, partner, 2),
            (replica_at(here, near, 0), replica_at(here, near, 0), 0),
        ]

    def sum_target(c):
        return partner if ROUTES[c] == "plane" else replica_at(here, 4 - ROUTES[c], 0)

    def send_rows(c):
        for owner, there, slot in sends(c):
            direct_route = ROUTES[c] == "direct"
            remote(
                rows.at[row_of(owner), part_of(c)], got.at[slot, part_of(c)],
                send_sem.at[1 if direct_route else 0],
                recv_sem.at[c, 1 if slot >= 3 and not direct_route else 0], there,
            ).start()

    def await_rows(c, stage, first, count):
        part = got.at[pl.ds(first, count), part_of(c)]
        remote(part, part, send_sem.at[0], recv_sem.at[c, stage], partner).wait_recv()

    def send_sum(c):
        await_rows(c, 1, 3, 3)
        there = sum_target(c)
        owner = row_of(there)

        def add(h, carry):
            part = pl.ds(pl.multiple_of(c * CHUNK + h * SUB, SUB), SUB)
            total = rows[owner, part, :].astype(jnp.float32)
            for k in range(3, 6):
                total = total + got[k, part, :].astype(jnp.float32)
            sum_out[part, :] = total
            return carry

        lax.fori_loop(0, CHUNK // SUB, add, 0)
        remote(
            sum_out.at[part_of(c)], sum_in.at[part_of(c)],
            send_sem.at[0], recv_sem.at[c, 0], there,
        ).start()

    for c in range(CHUNKS):
        split_rows(c)
        if c == 0:
            pl.semaphore_wait(barrier, len(peers) + len(neighbours))
        send_rows(c)

    for copy in state_loads:
        copy.wait()

    def onehot(c):
        tensor = lax.broadcasted_iota(jnp.int32, (TENSORS, CHUNK), 0)
        return (tensor == ids[pl.ds(c, 1), :]).astype(jnp.float32)

    sums[...] = jnp.zeros_like(sums)
    wide = lax.broadcasted_iota(jnp.int32, (2 * TENSORS, LANES), 0)
    lane = lax.broadcasted_iota(jnp.int32, (2 * TENSORS, LANES), 1)
    upper = wide < TENSORS
    tensor_of = jnp.where(upper, wide, wide - TENSORS)

    def index_blocks(c, carry):
        chosen = (tensor_of == ids[pl.ds(c, 1), :]).astype(jnp.float32)
        picks[pl.ds(pl.multiple_of(c * CHUNK, CHUNK), CHUNK), :] = chosen.T.astype(jnp.bfloat16)
        return carry

    lax.fori_loop(0, CHUNKS, index_blocks, 0)

    def weigh(c, carry):
        values = master[pl.ds(pl.multiple_of(c * CHUNK, CHUNK), CHUNK), :]
        sums[:TENSORS, :] += jnp.dot(
            onehot(c), values * values, precision=HIGH, preferred_element_type=jnp.float32
        )
        return carry

    lax.fori_loop(0, CHUNKS, weigh, 0)

    def step_chunk(c):
        direct_route = ROUTES[c] == "direct"
        await_rows(c, 0, 0, 7 if direct_route else 5)

        def step(h, carry):
            part = pl.ds(pl.multiple_of(c * CHUNK + h * SUB, SUB), SUB)
            total = rows[me, part, :].astype(jnp.float32)
            for k in range(7 if direct_route else 3):
                total = total + got[k, part, :].astype(jnp.float32)
            if not direct_route:
                total = total + sum_in[part, :]
            grad = total / REPLICAS
            next_moment = 0.9 * moment[part, :] + 0.1 * grad
            next_second = 0.999 * second[part, :] + 0.001 * grad * grad
            change = (
                next_moment / first_fix / (jnp.sqrt(next_second / second_fix) + tiny_eps)
                + decay_rate * master[part, :]
            )
            moment[part, :] = next_moment
            second[part, :] = next_second
            update[part, :] = change
            squares[pl.ds(pl.multiple_of(h * SUB, SUB), SUB), :] = change * change
            return carry

        lax.fori_loop(0, CHUNK // SUB, step, 0)
        sums[TENSORS:, :] += jnp.dot(
            onehot(c), squares[...], precision=HIGH, preferred_element_type=jnp.float32
        )

    for c in range(CHUNKS + LAG):
        if c in SUMMED:
            send_sum(c)
        if c >= LAG:
            step_chunk(c - LAG)

    per_tensor = jnp.sum(sums[...], axis=1, keepdims=True)
    mine[...] = jnp.broadcast_to(
        jnp.sum(jnp.where(wide == lane, per_tensor, 0.0), axis=0, keepdims=True), (8, LANES)
    )
    swaps = [
        remote(mine, theirs.at[i], sum_send, sum_recv, neighbours[len(OFFSETS) - 1 - i])
        for i in range(len(OFFSETS))
    ]
    for copy in swaps:
        copy.start()
    all_swaps = remote(theirs, theirs, sum_send, sum_recv, neighbours[0])
    all_swaps.wait_recv()
    total = mine[...]
    for i in range(len(OFFSETS)):
        total = total + theirs[i]
    trust = jnp.sqrt(total) / (jnp.sqrt(pltpu.roll(total, TENSORS, 1)) + tiny_eps)
    trust_row = trust[:1, :]
    trust_of = jnp.sum(jnp.where(tensor_of == lane, trust_row, 0.0), axis=1, keepdims=True)
    trust_of = jnp.broadcast_to(trust_of, (2 * TENSORS, LANES))
    high = trust_of.astype(jnp.bfloat16).astype(jnp.float32)
    middle = (trust_of - high).astype(jnp.bfloat16).astype(jnp.float32)
    low = trust_of - high - middle
    first_terms = jnp.where(upper, high, middle).astype(jnp.bfloat16)
    last_term = jnp.where(upper, low, 0.0).astype(jnp.bfloat16)

    beside = [replica_at(here, a, 0) for a in X_STEPS]
    behind = [replica_at(here, 4 - a, 0) for a in X_STEPS]
    direct_to = [partner] + beside

    def piece_of(p):
        return pl.ds(pl.multiple_of(p * PIECE, PIECE), PIECE)

    def direct(p, i):
        block = gathered.at[me, piece_of(p)]
        if p in Z_FIRST:
            sem = 0 if i == 0 else 1
        else:
            sem = (2, 0, 0, 1)[i]
        return remote(block, block, out_send, out_recv.at[3 * p + sem], direct_to[i])

    def onward_x(p, j):
        block = gathered.at[row_of(partner), piece_of(p)]
        return remote(block, block, out_send, out_recv.at[3 * p + 1], beside[j])

    def onward_z(p, j):
        block = gathered.at[row_of(behind[j]), piece_of(p)]
        return remote(block, block, out_send, out_recv.at[3 * p + 2], partner)

    def await_pieces(p, sem, count):
        blocks = got.at[pl.ds(0, count), piece_of(p)]
        remote(blocks, blocks, out_send, out_recv.at[3 * p + sem], partner).wait_recv()

    def finish_piece(p):
        part = pl.ds(p * PIECE, PIECE)
        pick = picks[part, :]
        trust_block = jnp.dot(
            pick, first_terms, preferred_element_type=jnp.float32
        ) + jnp.dot(pick, last_term, preferred_element_type=jnp.float32)
        new_master = master[part, :] - learn_rate * (update[part, :] * trust_block)
        master[part, :] = new_master
        gathered[me, part, :] = new_master.astype(jnp.bfloat16)

    def forward_x(p):
        await_pieces(p, 0, 1)
        for j in range(3):
            onward_x(p, j).start()

    def forward_z(p):
        await_pieces(p, 0, 2)
        onward_z(p, 0).start()
        onward_z(p, 1).start()
        await_pieces(p, 1, 1)
        onward_z(p, 2).start()

    def collect(p):
        if p in Z_FIRST:
            await_pieces(p, 1, 6)
        else:
            await_pieces(p, 2, 4)
        for r in range(REPLICAS):
            spread[pl.ds(r, PIECE, stride=8), :] = gathered[r, piece_of(p), :].astype(jnp.float32)

        def tile(t, carry):
            for i in range(8):
                at = t * 8 + i
                cols = pl.ds(pl.multiple_of((p * PIECE + at) * LANES, LANES), LANES)
                packed[:, cols] = spread[pl.ds(pl.multiple_of(at * 8, 8), 8), :].astype(
                    jnp.bfloat16
                )
            return carry

        lax.fori_loop(0, PIECE // 8, tile, 0)

    for p in range(PIECES):
        finish_piece(p)
        if p in Z_FIRST:
            direct(p, 0).start()
        else:
            for i in range(1, 4):
                direct(p, i).start()
    for p in X_FIRST:
        direct(p, 0).start()
    for k in range(max(len(Z_FIRST), len(X_FIRST))):
        if k < len(Z_FIRST):
            for i in range(1, 4):
                direct(Z_FIRST[k], i).start()
        if k < len(X_FIRST):
            forward_z(X_FIRST[k])
        if k < len(Z_FIRST):
            forward_x(Z_FIRST[k])
    for p in X_FIRST + Z_FIRST:
        collect(p)

    shared = rows.at[:, pl.ds(0, len(SUMMED) * CHUNK)]
    remote(shared, shared, send_sem.at[0], recv_sem.at[0, 0], partner).wait_send()
    for c in range(CHUNKS):
        if c not in SUMMED:
            straight = got.at[:, part_of(c)]
            remote(straight, straight, send_sem.at[1], recv_sem.at[c, 0], partner).wait_send()
    remote(theirs, theirs, sum_send, sum_recv, partner).wait_send()
    remote(got, got, out_send, out_recv.at[0], partner).wait_send()


def hand_over(*refs):
    sem = refs[-1]
    copies = [pltpu.make_async_copy(refs[i], refs[4 + i], sem.at[i]) for i in range(4)]
    for copy in copies:
        copy.start()
    for copy in copies:
        copy.wait()


def on_device(gradients, master, moment, second, segment_ids):
    flat = master.shape[0]
    tall = (BLOCKS, LANES)
    f32, bf16 = jnp.float32, jnp.bfloat16
    vmem_spec = pl.BlockSpec(memory_space=pltpu.VMEM)
    dma = pltpu.SemaphoreType.DMA
    weights, new_master, new_moment, new_second = pl.pallas_call(
        kernel,
        out_shape=(
            jax.ShapeDtypeStruct((REPLICAS, flat), bf16),
            jax.ShapeDtypeStruct(tall, f32),
            jax.ShapeDtypeStruct(tall, f32),
            jax.ShapeDtypeStruct(tall, f32),
        ),
        in_specs=[pl.BlockSpec(memory_space=pltpu.HBM)] * 5,
        out_specs=(vmem_spec,) * 4,
        scratch_shapes=[
            pltpu.VMEM((REPLICAS, flat), bf16),
            pltpu.VMEM((REPLICAS, BLOCKS, LANES), bf16),
            pltpu.VMEM((len(STEPS), BLOCKS, LANES), bf16),
            pltpu.VMEM(tall, f32),
            pltpu.VMEM(tall, f32),
            pltpu.VMEM(tall, f32),
            pltpu.VMEM((CHUNKS, CHUNK), jnp.int32),
            pltpu.VMEM((BLOCKS, LANES), bf16),
            pltpu.VMEM((CHUNK, LANES), f32),
            pltpu.VMEM((2 * TENSORS, LANES), f32),
            pltpu.VMEM((8, LANES), f32),
            pltpu.VMEM((len(OFFSETS), 8, LANES), f32),
            pltpu.VMEM((CHUNK * 8, LANES), f32),
            pltpu.VMEM((REPLICAS, BLOCKS, LANES), bf16),
            dma((CHUNKS,)),
            dma((4,)),
            dma((2,)),
            dma((CHUNKS, 2)),
            dma,
            dma,
            dma,
            dma((PIECES * 3,)),
        ],
        compiler_params=pltpu.CompilerParams(
            collective_id=0, has_side_effects=True, vmem_limit_bytes=40 << 20
        ),
        name="lamb_step",
    )(
        *(
            pltpu.with_memory_space_constraint(array, pltpu.HBM)
            for array in (
                gradients.reshape(REPLICAS, flat),
                master.reshape(tall),
                moment.reshape(tall),
                second.reshape(tall),
                segment_ids.reshape(CHUNKS, CHUNK),
            )
        )
    )
    weights, new_master, new_moment, new_second = pl.pallas_call(
        hand_over,
        out_shape=(
            jax.ShapeDtypeStruct((REPLICAS, flat), bf16),
            jax.ShapeDtypeStruct(tall, f32),
            jax.ShapeDtypeStruct(tall, f32),
            jax.ShapeDtypeStruct(tall, f32),
        ),
        in_specs=[vmem_spec] * 4,
        out_specs=(pl.BlockSpec(memory_space=pltpu.HBM),) * 4,
        scratch_shapes=[dma((4,))],
        compiler_params=pltpu.CompilerParams(vmem_limit_bytes=8 << 20),
        name="hand_over",
    )(weights, new_master, new_moment, new_second)
    return (weights, new_master.reshape(-1), new_moment.reshape(-1), new_second.reshape(-1))


def solution(mesh):
    torus = Mesh(mesh.devices.reshape(2, 4, 4, 2, 2), AXES)
    return jax.shard_map(
        on_device,
        mesh=torus,
        in_specs=(P(DP, None, SHARD), P(DP_SHARD), P(DP_SHARD), P(DP_SHARD), P(DP_SHARD)),
        out_specs=(P(None, SHARD), P(DP_SHARD), P(DP_SHARD), P(DP_SHARD)),
        check_vma=False,
    )
```

```python
import functools

import jax
import jax.numpy as jnp
from jax import lax
from jax.experimental import pallas as pl
from jax.experimental.pallas import tpu as pltpu
from jax.sharding import Mesh
from jax.sharding import PartitionSpec as P

AXES = ("zh", "x", "y", "zl", "core")
DP = ("zh", "x")
SHARD = ("y", "zl", "core")
DP_SHARD = AXES
MESH = pl.DeviceIdType.MESH

first_fix = 1.0 - 0.9**20
second_fix = 1.0 - 0.999**20
learn_rate = 0.2
decay_rate = 0.01
tiny_eps = 1e-06

REPLICAS = 8
TENSORS = 64
BLOCKS = 768
LANES = 128
CHUNK = 128
CHUNKS = BLOCKS // CHUNK
SUB = 32
PIECE = 64
PIECES = BLOCKS // PIECE
REACH = 4
Z_FIRST = (0, 2, 4, 6, 8, 10)
X_FIRST = tuple(p for p in range(PIECES) if p not in Z_FIRST)
LAG = 3
HIGH = lax.Precision.HIGHEST

STEPS = ((1, 1), (3, 0), (2, 1), (1, 0), (0, 1), (3, 1), (2, 0))
X_STEPS = (1, 3, 2)
ROUTES = ("plane", "plane", 1, 3, "direct", "direct")
SUMMED = tuple(c for c in range(CHUNKS) if ROUTES[c] != "direct")
OFFSETS = tuple(range(-REACH, 0)) + tuple(range(1, REACH + 1))


def place():
    return {axis: lax.axis_index(axis) for axis in AXES}


def replica_at(here, x_step, z_step):
    there = dict(here)
    there["x"] = lax.rem(here["x"] + x_step, 4)
    there["zh"] = lax.rem(here["zh"] + z_step, 2)
    return there


def row_of(there):
    return there["zh"] * 4 + there["x"]


def flat_neighbour(here, offset):
    rank = (((here["zh"] * 4 + here["x"]) * 4 + here["y"]) * 2 + here["zl"]) * 2 + here["core"]
    rank = lax.rem(rank + offset + 128, 128)
    return {
        "zh": rank // 64,
        "x": lax.rem(rank // 16, 4),
        "y": lax.rem(rank // 4, 4),
        "zl": lax.rem(rank // 2, 2),
        "core": lax.rem(rank, 2),
    }


def remote(src, dst, send_sem, recv_sem, there):
    return pltpu.make_async_remote_copy(
        src_ref=src,
        dst_ref=dst,
        send_sem=send_sem,
        recv_sem=recv_sem,
        device_id=there,
        device_id_type=MESH,
    )


def kernel(
    grad_hbm, master_hbm, moment_hbm, second_hbm, ids_hbm,
    packed, master, moment, second,
    grad_in, rows, got, sum_out, sum_in, update, ids, picks, squares, sums,
    mine, theirs, spread, gathered,
    load_sem, state_sem, send_sem, recv_sem, sum_send, sum_recv,
    out_send, out_recv,
):
    here = place()
    me = row_of(here)
    peers = [replica_at(here, a, b) for a, b in STEPS]
    neighbours = [flat_neighbour(here, k) for k in OFFSETS]

    barrier = pltpu.get_barrier_semaphore()
    for there in peers + neighbours:
        pl.semaphore_signal(barrier, inc=1, device_id=there, device_id_type=MESH)

    def load(c):
        cols = pl.ds(pl.multiple_of(c * CHUNK * LANES, CHUNK * LANES), CHUNK * LANES)
        return pltpu.make_async_copy(grad_hbm.at[:, cols], grad_in.at[:, cols], load_sem.at[c])

    for c in range(CHUNKS):
        load(c).start()
    state_loads = [
        pltpu.make_async_copy(src, dst, state_sem.at[i])
        for i, (src, dst) in enumerate(
            ((ids_hbm, ids), (master_hbm, master), (moment_hbm, moment), (second_hbm, second))
        )
    ]
    for copy in state_loads:
        copy.start()

    def split_rows(c):
        load(c).wait()

        def tile(t, carry):
            at = c * CHUNK + t * 8
            for i in range(8):
                cols = pl.ds(pl.multiple_of((at + i) * LANES, LANES), LANES)
                spread[pl.ds(pl.multiple_of((t * 8 + i) * 8, 8), 8), :] = grad_in[:, cols].astype(
                    jnp.float32
                )
            return carry

        lax.fori_loop(0, CHUNK // 8, tile, 0)
        for r in range(REPLICAS):
            for h in range(CHUNK // SUB):
                piece = spread[pl.ds(h * SUB * 8 + r, SUB, stride=8), :]
                rows[r, pl.ds(pl.multiple_of(c * CHUNK + h * SUB, SUB), SUB), :] = piece.astype(
                    jnp.bfloat16
                )

    def part_of(c):
        return pl.ds(c * CHUNK, CHUNK)

    partner = replica_at(here, 0, 1)

    def sends(c):
        route = ROUTES[c]
        if route == "direct":
            return [(there, there, k) for k, there in enumerate(peers)]
        if route == "plane":
            out = []
            for j, a in enumerate(X_STEPS):
                there = replica_at(here, a, 0)
                out.append((replica_at(here, a, 1), there, 3 + j))
                out.append((there, there, j))
            return out
        near, back = route, 4 - route
        return [
            (replica_at(here, 2, 1), replica_at(here, back, 1), 4),
            (replica_at(here, 2, 0), replica_at(here, back, 0), 3),
            (replica_at(here, back, 1), partner, 5),
            (replica_at(here, near, 1), replica_at(here, near, 1), 1),
            (partner, partner, 2),
            (replica_at(here, near, 0), replica_at(here, near, 0), 0),
        ]

    def sum_target(c):
        return partner if ROUTES[c] == "plane" else replica_at(here, 4 - ROUTES[c], 0)

    def send_rows(c):
        for owner, there, at in sends(c):
            direct_route = ROUTES[c] == "direct"
            remote(
                rows.at[row_of(owner), part_of(c)], got.at[at, part_of(c)],
                send_sem.at[1 if direct_route else 0],
                recv_sem.at[CHUNKS + SUMMED.index(c) if at >= 3 and not direct_route else c], there,
            ).start()

    def await_rows(c, stage, first, count):
        part = got.at[pl.ds(first, count), part_of(c)]
        remote(part, part, send_sem.at[0], recv_sem.at[CHUNKS + SUMMED.index(c) if stage else c], partner).wait_recv()

    def send_sum(c):
        await_rows(c, 1, 3, 3)
        there = sum_target(c)
        owner = row_of(there)

        def add(h, carry):
            part = pl.ds(pl.multiple_of(c * CHUNK + h * SUB, SUB), SUB)
            total = rows[owner, part, :].astype(jnp.float32)
            for k in range(3, 6):
                total = total + got[k, part, :].astype(jnp.float32)
            sum_out[part, :] = total
            return carry

        lax.fori_loop(0, CHUNK // SUB, add, 0)
        remote(
            sum_out.at[part_of(c)], sum_in.at[part_of(c)],
            send_sem.at[0], recv_sem.at[c], there,
        ).start()

    for c in range(CHUNKS):
        split_rows(c)
        if c == 0:
            pl.semaphore_wait(barrier, len(peers) + len(neighbours))
        send_rows(c)

    for copy in state_loads:
        copy.wait()

    def onehot(c):
        tensor = lax.broadcasted_iota(jnp.int32, (TENSORS, CHUNK), 0)
        return (tensor == ids[pl.ds(c, 1), :]).astype(jnp.float32)

    sums[...] = jnp.zeros_like(sums)
    wide = lax.broadcasted_iota(jnp.int32, (2 * TENSORS, LANES), 0)
    lane = lax.broadcasted_iota(jnp.int32, (2 * TENSORS, LANES), 1)
    upper = wide < TENSORS
    tensor_of = jnp.where(upper, wide, wide - TENSORS)

    def index_blocks(c, carry):
        chosen = (tensor_of == ids[pl.ds(c, 1), :]).astype(jnp.float32)
        picks[pl.ds(pl.multiple_of(c * CHUNK, CHUNK), CHUNK), :] = chosen.T.astype(jnp.bfloat16)
        return carry

    lax.fori_loop(0, CHUNKS, index_blocks, 0)

    def weigh(c, carry):
        values = master[pl.ds(pl.multiple_of(c * CHUNK, CHUNK), CHUNK), :]
        sums[:TENSORS, :] += jnp.dot(
            onehot(c), values * values, precision=HIGH, preferred_element_type=jnp.float32
        )
        return carry

    lax.fori_loop(0, CHUNKS, weigh, 0)

    def step_chunk(c):
        direct_route = ROUTES[c] == "direct"
        await_rows(c, 0, 0, 7 if direct_route else 5)

        def step(h, carry):
            part = pl.ds(pl.multiple_of(c * CHUNK + h * SUB, SUB), SUB)
            total = rows[me, part, :].astype(jnp.float32)
            for k in range(7 if direct_route else 3):
                total = total + got[k, part, :].astype(jnp.float32)
            if not direct_route:
                total = total + sum_in[part, :]
            grad = total / REPLICAS
            next_moment = 0.9 * moment[part, :] + 0.1 * grad
            next_second = 0.999 * second[part, :] + 0.001 * grad * grad
            change = (
                next_moment / first_fix / (jnp.sqrt(next_second / second_fix) + tiny_eps)
                + decay_rate * master[part, :]
            )
            moment[part, :] = next_moment
            second[part, :] = next_second
            update[part, :] = change
            squares[pl.ds(pl.multiple_of(h * SUB, SUB), SUB), :] = change * change
            return carry

        lax.fori_loop(0, CHUNK // SUB, step, 0)
        sums[TENSORS:, :] += jnp.dot(
            onehot(c), squares[...], precision=HIGH, preferred_element_type=jnp.float32
        )

    for c in range(CHUNKS + LAG):
        if c in SUMMED:
            send_sum(c)
        if c >= LAG:
            step_chunk(c - LAG)

    per_tensor = jnp.sum(sums[...], axis=1, keepdims=True)
    mine[...] = jnp.broadcast_to(
        jnp.sum(jnp.where(wide == lane, per_tensor, 0.0), axis=0, keepdims=True), (8, LANES)
    )
    swaps = [
        remote(mine.at[pl.ds(0, 1)], theirs.at[pl.ds(i, 1)], sum_send, sum_recv, neighbours[len(OFFSETS) - 1 - i])
        for i in range(len(OFFSETS))
    ]
    for copy in swaps:
        copy.start()
    all_swaps = remote(theirs, theirs, sum_send, sum_recv, neighbours[0])
    all_swaps.wait_recv()
    total = mine[...] + jnp.sum(theirs[...], axis=0, keepdims=True)
    trust = jnp.sqrt(total) / (jnp.sqrt(pltpu.roll(total, TENSORS, 1)) + tiny_eps)
    trust_row = trust[:1, :]
    trust_of = jnp.sum(jnp.where(tensor_of == lane, trust_row, 0.0), axis=1, keepdims=True)
    trust_of = jnp.broadcast_to(trust_of, (2 * TENSORS, LANES))
    high = trust_of.astype(jnp.bfloat16).astype(jnp.float32)
    middle = (trust_of - high).astype(jnp.bfloat16).astype(jnp.float32)
    low = trust_of - high - middle
    first_terms = jnp.where(upper, high, middle).astype(jnp.bfloat16)
    last_term = jnp.where(upper, low, 0.0).astype(jnp.bfloat16)

    beside = [replica_at(here, a, 0) for a in X_STEPS]
    behind = [replica_at(here, 4 - a, 0) for a in X_STEPS]
    direct_to = [partner] + beside

    def piece_of(p):
        return pl.ds(pl.multiple_of(p * PIECE, PIECE), PIECE)

    def slot(p):
        if p in Z_FIRST:
            return 2 * Z_FIRST.index(p)
        return 2 * len(Z_FIRST) + 3 * X_FIRST.index(p)

    def direct(p, i):
        block = gathered.at[me, piece_of(p)]
        if p in Z_FIRST:
            sem = 0 if i == 0 else 1
        else:
            sem = (2, 0, 0, 1)[i]
        return remote(block, block, out_send, out_recv.at[slot(p) + sem], direct_to[i])

    def onward_x(p, j):
        block = gathered.at[row_of(partner), piece_of(p)]
        return remote(block, block, out_send, out_recv.at[slot(p) + 1], beside[j])

    def onward_z(p, j):
        block = gathered.at[row_of(behind[j]), piece_of(p)]
        return remote(block, block, out_send, out_recv.at[slot(p) + 2], partner)

    def await_pieces(p, sem, count):
        blocks = got.at[pl.ds(0, count), piece_of(p)]
        remote(blocks, blocks, out_send, out_recv.at[slot(p) + sem], partner).wait_recv()

    def finish_piece(p):
        part = pl.ds(p * PIECE, PIECE)
        pick = picks[part, :]
        trust_block = jnp.dot(
            pick, first_terms, preferred_element_type=jnp.float32
        ) + jnp.dot(pick, last_term, preferred_element_type=jnp.float32)
        new_master = master[part, :] - learn_rate * (update[part, :] * trust_block)
        master[part, :] = new_master
        gathered[me, part, :] = new_master.astype(jnp.bfloat16)

    def forward_x(p):
        await_pieces(p, 0, 1)
        for j in range(3):
            onward_x(p, j).start()

    def forward_z(p):
        await_pieces(p, 0, 2)
        onward_z(p, 0).start()
        onward_z(p, 1).start()
        await_pieces(p, 1, 1)
        onward_z(p, 2).start()

    def collect(p):
        if p in Z_FIRST:
            await_pieces(p, 1, 6)
        else:
            await_pieces(p, 2, 4)
        for r in range(REPLICAS):
            spread[pl.ds(r, PIECE, stride=8), :] = gathered[r, piece_of(p), :].astype(jnp.float32)

        def tile(t, carry):
            for i in range(8):
                at = t * 8 + i
                cols = pl.ds(pl.multiple_of((p * PIECE + at) * LANES, LANES), LANES)
                packed[:, cols] = spread[pl.ds(pl.multiple_of(at * 8, 8), 8), :].astype(
                    jnp.bfloat16
                )
            return carry

        lax.fori_loop(0, PIECE // 8, tile, 0)

    for p in range(PIECES):
        finish_piece(p)
        if p in Z_FIRST:
            direct(p, 0).start()
        else:
            for i in range(1, 4):
                direct(p, i).start()
    for p in X_FIRST:
        direct(p, 0).start()
    for k in range(max(len(Z_FIRST), len(X_FIRST))):
        if k < len(Z_FIRST):
            for i in range(1, 4):
                direct(Z_FIRST[k], i).start()
        if k < len(X_FIRST):
            forward_z(X_FIRST[k])
        if k < len(Z_FIRST):
            forward_x(Z_FIRST[k])
    for p in X_FIRST + Z_FIRST:
        collect(p)

    shared = rows.at[:, pl.ds(0, len(SUMMED) * CHUNK)]
    remote(shared, shared, send_sem.at[0], recv_sem.at[0], partner).wait_send()
    for c in range(CHUNKS):
        if c not in SUMMED:
            straight = got.at[:, part_of(c)]
            remote(straight, straight, send_sem.at[1], recv_sem.at[c], partner).wait_send()
    remote(theirs, theirs, sum_send, sum_recv, partner).wait_send()
    remote(got, got, out_send, out_recv.at[0], partner).wait_send()


def hand_over(*refs):
    sem = refs[-1]
    copies = [pltpu.make_async_copy(refs[i], refs[4 + i], sem.at[i]) for i in range(4)]
    for copy in copies:
        copy.start()
    for copy in copies:
        copy.wait()


def on_device(gradients, master, moment, second, segment_ids):
    flat = master.shape[0]
    tall = (BLOCKS, LANES)
    f32, bf16 = jnp.float32, jnp.bfloat16
    vmem_spec = pl.BlockSpec(memory_space=pltpu.VMEM)
    dma = pltpu.SemaphoreType.DMA
    weights, new_master, new_moment, new_second = pl.pallas_call(
        kernel,
        out_shape=(
            jax.ShapeDtypeStruct((REPLICAS, flat), bf16),
            jax.ShapeDtypeStruct(tall, f32),
            jax.ShapeDtypeStruct(tall, f32),
            jax.ShapeDtypeStruct(tall, f32),
        ),
        in_specs=[pl.BlockSpec(memory_space=pltpu.HBM)] * 5,
        out_specs=(vmem_spec,) * 4,
        scratch_shapes=[
            pltpu.VMEM((REPLICAS, flat), bf16),
            pltpu.VMEM((REPLICAS, BLOCKS, LANES), bf16),
            pltpu.VMEM((len(STEPS), BLOCKS, LANES), bf16),
            pltpu.VMEM(tall, f32),
            pltpu.VMEM(tall, f32),
            pltpu.VMEM(tall, f32),
            pltpu.VMEM((CHUNKS, CHUNK), jnp.int32),
            pltpu.VMEM((BLOCKS, LANES), bf16),
            pltpu.VMEM((CHUNK, LANES), f32),
            pltpu.VMEM((2 * TENSORS, LANES), f32),
            pltpu.VMEM((8, LANES), f32),
            pltpu.VMEM((len(OFFSETS), LANES), f32),
            pltpu.VMEM((CHUNK * 8, LANES), f32),
            pltpu.VMEM((REPLICAS, BLOCKS, LANES), bf16),
            dma((CHUNKS,)),
            dma((4,)),
            dma((2,)),
            dma((CHUNKS + len(SUMMED),)),
            dma,
            dma,
            dma,
            dma((len(X_FIRST) * 3 + len(Z_FIRST) * 2,)),
        ],
        compiler_params=pltpu.CompilerParams(
            collective_id=0, has_side_effects=True, vmem_limit_bytes=40 << 20
        ),
        name="lamb_step",
    )(
        *(
            pltpu.with_memory_space_constraint(array, pltpu.HBM)
            for array in (
                gradients.reshape(REPLICAS, flat),
                master.reshape(tall),
                moment.reshape(tall),
                second.reshape(tall),
                segment_ids.reshape(CHUNKS, CHUNK),
            )
        )
    )
    weights, new_master, new_moment, new_second = pl.pallas_call(
        hand_over,
        out_shape=(
            jax.ShapeDtypeStruct((REPLICAS, flat), bf16),
            jax.ShapeDtypeStruct(tall, f32),
            jax.ShapeDtypeStruct(tall, f32),
            jax.ShapeDtypeStruct(tall, f32),
        ),
        in_specs=[vmem_spec] * 4,
        out_specs=(pl.BlockSpec(memory_space=pltpu.HBM),) * 4,
        scratch_shapes=[dma((4,))],
        compiler_params=pltpu.CompilerParams(vmem_limit_bytes=8 << 20),
        name="hand_over",
    )(weights, new_master, new_moment, new_second)
    return (weights, new_master.reshape(-1), new_moment.reshape(-1), new_second.reshape(-1))


def solution(mesh):
    torus = Mesh(mesh.devices.reshape(2, 4, 4, 2, 2), AXES)
    return jax.shard_map(
        on_device,
        mesh=torus,
        in_specs=(P(DP, None, SHARD), P(DP_SHARD), P(DP_SHARD), P(DP_SHARD), P(DP_SHARD)),
        out_specs=(P(None, SHARD), P(DP_SHARD), P(DP_SHARD), P(DP_SHARD)),
        check_vma=False,
    )
```

```python
import functools

import jax
import jax.numpy as jnp
from jax import lax
from jax.experimental import pallas as pl
from jax.experimental.pallas import tpu as pltpu
from jax.sharding import Mesh
from jax.sharding import PartitionSpec as P

AXES = ("zh", "x", "y", "zl", "core")
DP = ("zh", "x")
SHARD = ("y", "zl", "core")
DP_SHARD = AXES
MESH = pl.DeviceIdType.MESH

first_fix = 1.0 - 0.9**20
second_fix = 1.0 - 0.999**20
learn_rate = 0.2
decay_rate = 0.01
tiny_eps = 1e-06

REPLICAS = 8
TENSORS = 64
BLOCKS = 768
LANES = 128
CHUNK = 128
CHUNKS = BLOCKS // CHUNK
SUB = 32
PIECE = 128
PIECES = BLOCKS // PIECE
REACH = 4
Z_FIRST = (0, 2, 4)
X_FIRST = tuple(p for p in range(PIECES) if p not in Z_FIRST)
LAG = 4
HIGH = lax.Precision.HIGHEST

STEPS = ((1, 1), (3, 0), (2, 1), (1, 0), (0, 1), (3, 1), (2, 0))
X_STEPS = (1, 3, 2)
ROUTES = ("plane", "plane", 1, 3, "direct", "direct")
SUMMED = tuple(c for c in range(CHUNKS) if ROUTES[c] != "direct")
OFFSETS = tuple(range(-REACH, 0)) + tuple(range(1, REACH + 1))


def place():
    return {axis: lax.axis_index(axis) for axis in AXES}


def replica_at(here, x_step, z_step):
    there = dict(here)
    there["x"] = lax.rem(here["x"] + x_step, 4)
    there["zh"] = lax.rem(here["zh"] + z_step, 2)
    return there


def row_of(there):
    return there["zh"] * 4 + there["x"]


def flat_neighbour(here, offset):
    rank = (((here["zh"] * 4 + here["x"]) * 4 + here["y"]) * 2 + here["zl"]) * 2 + here["core"]
    rank = lax.rem(rank + offset + 128, 128)
    return {
        "zh": rank // 64,
        "x": lax.rem(rank // 16, 4),
        "y": lax.rem(rank // 4, 4),
        "zl": lax.rem(rank // 2, 2),
        "core": lax.rem(rank, 2),
    }


def remote(src, dst, send_sem, recv_sem, there):
    return pltpu.make_async_remote_copy(
        src_ref=src,
        dst_ref=dst,
        send_sem=send_sem,
        recv_sem=recv_sem,
        device_id=there,
        device_id_type=MESH,
    )


def kernel(
    grad_hbm, master_hbm, moment_hbm, second_hbm, ids_hbm,
    packed, master, moment, second,
    grad_in, rows, got, sum_out, sum_in, update, ids, picks, squares, sums,
    mine, theirs, spread, gathered,
    load_sem, state_sem, send_sem, recv_sem, sum_send, sum_recv,
    out_send, out_recv,
):
    here = place()
    me = row_of(here)
    peers = [replica_at(here, a, b) for a, b in STEPS]
    neighbours = [flat_neighbour(here, k) for k in OFFSETS]

    barrier = pltpu.get_barrier_semaphore()
    for there in peers + neighbours:
        pl.semaphore_signal(barrier, inc=1, device_id=there, device_id_type=MESH)

    def load(c):
        cols = pl.ds(pl.multiple_of(c * CHUNK * LANES, CHUNK * LANES), CHUNK * LANES)
        return pltpu.make_async_copy(grad_hbm.at[:, cols], grad_in.at[:, cols], load_sem.at[c])

    for c in range(CHUNKS):
        load(c).start()
    state_loads = [
        pltpu.make_async_copy(src, dst, state_sem.at[i])
        for i, (src, dst) in enumerate(
            ((ids_hbm, ids), (master_hbm, master), (moment_hbm, moment), (second_hbm, second))
        )
    ]
    for copy in state_loads:
        copy.start()

    def split_rows(c):
        load(c).wait()

        def tile(t, carry):
            at = c * CHUNK + t * 8
            for i in range(8):
                cols = pl.ds(pl.multiple_of((at + i) * LANES, LANES), LANES)
                spread[pl.ds(pl.multiple_of((t * 8 + i) * 8, 8), 8), :] = grad_in[:, cols].astype(
                    jnp.float32
                )
            return carry

        lax.fori_loop(0, CHUNK // 8, tile, 0)
        for r in range(REPLICAS):
            for h in range(CHUNK // SUB):
                piece = spread[pl.ds(h * SUB * 8 + r, SUB, stride=8), :]
                rows[r, pl.ds(pl.multiple_of(c * CHUNK + h * SUB, SUB), SUB), :] = piece.astype(
                    jnp.bfloat16
                )

    def part_of(c):
        return pl.ds(c * CHUNK, CHUNK)

    partner = replica_at(here, 0, 1)

    def sends(c):
        route = ROUTES[c]
        if route == "direct":
            return [(there, there, k) for k, there in enumerate(peers)]
        if route == "plane":
            out = []
            for j, a in enumerate(X_STEPS):
                there = replica_at(here, a, 0)
                out.append((replica_at(here, a, 1), there, 3 + j))
                out.append((there, there, j))
            return out
        near, back = route, 4 - route
        return [
            (replica_at(here, 2, 1), replica_at(here, back, 1), 4),
            (replica_at(here, 2, 0), replica_at(here, back, 0), 3),
            (replica_at(here, back, 1), partner, 5),
            (replica_at(here, near, 1), replica_at(here, near, 1), 1),
            (partner, partner, 2),
            (replica_at(here, near, 0), replica_at(here, near, 0), 0),
        ]

    def sum_target(c):
        return partner if ROUTES[c] == "plane" else replica_at(here, 4 - ROUTES[c], 0)

    def send_rows(c):
        for owner, there, at in sends(c):
            direct_route = ROUTES[c] == "direct"
            remote(
                rows.at[row_of(owner), part_of(c)], got.at[at, part_of(c)],
                send_sem.at[1 if direct_route else 0],
                recv_sem.at[CHUNKS + SUMMED.index(c) if at >= 3 and not direct_route else c], there,
            ).start()

    def await_rows(c, stage, first, count):
        part = got.at[pl.ds(first, count), part_of(c)]
        remote(part, part, send_sem.at[0], recv_sem.at[CHUNKS + SUMMED.index(c) if stage else c], partner).wait_recv()

    def send_sum(c):
        await_rows(c, 1, 3, 3)
        there = sum_target(c)
        owner = row_of(there)

        def add(h, carry):
            part = pl.ds(pl.multiple_of(c * CHUNK + h * SUB, SUB), SUB)
            total = rows[owner, part, :].astype(jnp.float32)
            for k in range(3, 6):
                total = total + got[k, part, :].astype(jnp.float32)
            sum_out[part, :] = total
            return carry

        lax.fori_loop(0, CHUNK // SUB, add, 0)
        remote(
            sum_out.at[part_of(c)], sum_in.at[part_of(c)],
            send_sem.at[0], recv_sem.at[c], there,
        ).start()

    for c in range(CHUNKS):
        split_rows(c)
        if c == 0:
            pl.semaphore_wait(barrier, len(peers) + len(neighbours))
        send_rows(c)

    for copy in state_loads:
        copy.wait()

    def onehot(c):
        tensor = lax.broadcasted_iota(jnp.int32, (TENSORS, CHUNK), 0)
        return (tensor == ids[pl.ds(c, 1), :]).astype(jnp.float32)

    sums[...] = jnp.zeros_like(sums)
    wide = lax.broadcasted_iota(jnp.int32, (2 * TENSORS, LANES), 0)
    lane = lax.broadcasted_iota(jnp.int32, (2 * TENSORS, LANES), 1)
    upper = wide < TENSORS
    tensor_of = jnp.where(upper, wide, wide - TENSORS)

    def index_blocks(c, carry):
        chosen = (tensor_of == ids[pl.ds(c, 1), :]).astype(jnp.float32)
        picks[pl.ds(pl.multiple_of(c * CHUNK, CHUNK), CHUNK), :] = chosen.T.astype(jnp.bfloat16)
        return carry

    lax.fori_loop(0, CHUNKS, index_blocks, 0)

    def weigh(c, carry):
        values = master[pl.ds(pl.multiple_of(c * CHUNK, CHUNK), CHUNK), :]
        sums[:TENSORS, :] += jnp.dot(
            onehot(c), values * values, precision=HIGH, preferred_element_type=jnp.float32
        )
        return carry

    lax.fori_loop(0, CHUNKS, weigh, 0)

    def step_chunk(c):
        direct_route = ROUTES[c] == "direct"
        await_rows(c, 0, 0, 7 if direct_route else 5)

        def step(h, carry):
            part = pl.ds(pl.multiple_of(c * CHUNK + h * SUB, SUB), SUB)
            total = rows[me, part, :].astype(jnp.float32)
            for k in range(7 if direct_route else 3):
                total = total + got[k, part, :].astype(jnp.float32)
            if not direct_route:
                total = total + sum_in[part, :]
            grad = total / REPLICAS
            next_moment = 0.9 * moment[part, :] + 0.1 * grad
            next_second = 0.999 * second[part, :] + 0.001 * grad * grad
            change = (
                next_moment / first_fix / (jnp.sqrt(next_second / second_fix) + tiny_eps)
                + decay_rate * master[part, :]
            )
            moment[part, :] = next_moment
            second[part, :] = next_second
            update[part, :] = change
            squares[pl.ds(pl.multiple_of(h * SUB, SUB), SUB), :] = change * change
            return carry

        lax.fori_loop(0, CHUNK // SUB, step, 0)
        sums[TENSORS:, :] += jnp.dot(
            onehot(c), squares[...], precision=HIGH, preferred_element_type=jnp.float32
        )

    for c in range(CHUNKS + LAG):
        if c in SUMMED:
            send_sum(c)
        if c >= LAG:
            step_chunk(c - LAG)

    per_tensor = jnp.sum(sums[...], axis=1, keepdims=True)
    mine[...] = jnp.broadcast_to(
        jnp.sum(jnp.where(wide == lane, per_tensor, 0.0), axis=0, keepdims=True), (8, LANES)
    )
    swaps = [
        remote(mine.at[pl.ds(0, 1)], theirs.at[pl.ds(i, 1)], sum_send, sum_recv, neighbours[len(OFFSETS) - 1 - i])
        for i in range(len(OFFSETS))
    ]
    for copy in swaps:
        copy.start()
    all_swaps = remote(theirs, theirs, sum_send, sum_recv, neighbours[0])
    all_swaps.wait_recv()
    total = mine[...] + jnp.sum(theirs[...], axis=0, keepdims=True)
    trust = jnp.sqrt(total) / (jnp.sqrt(pltpu.roll(total, TENSORS, 1)) + tiny_eps)
    trust_row = trust[:1, :]
    trust_of = jnp.sum(jnp.where(tensor_of == lane, trust_row, 0.0), axis=1, keepdims=True)
    trust_of = jnp.broadcast_to(trust_of, (2 * TENSORS, LANES))
    high = trust_of.astype(jnp.bfloat16).astype(jnp.float32)
    middle = (trust_of - high).astype(jnp.bfloat16).astype(jnp.float32)
    low = trust_of - high - middle
    first_terms = jnp.where(upper, high, middle).astype(jnp.bfloat16)
    last_term = jnp.where(upper, low, 0.0).astype(jnp.bfloat16)

    beside = [replica_at(here, a, 0) for a in X_STEPS]
    behind = [replica_at(here, 4 - a, 0) for a in X_STEPS]
    direct_to = [partner] + beside

    def piece_of(p):
        return pl.ds(pl.multiple_of(p * PIECE, PIECE), PIECE)

    def slot(p):
        return 3 * p

    def direct(p, i):
        block = gathered.at[me, piece_of(p)]
        if p in Z_FIRST:
            sem = (0, 1 + Z_FIRST.index(p) % 2, 2 - Z_FIRST.index(p) % 2)[i]
        else:
            sem = (2, 0, 0, 1)[i]
        return remote(block, block, out_send, out_recv.at[slot(p) + sem], direct_to[i])

    def relay(p):
        turn = Z_FIRST.index(p) % 2
        block = gathered.at[row_of(behind[turn]), piece_of(p)]
        return remote(block, block, out_send, out_recv.at[slot(p) + 2], beside[turn])

    def onward_x(p, j):
        block = gathered.at[row_of(partner), piece_of(p)]
        return remote(block, block, out_send, out_recv.at[slot(p) + 2], beside[j])

    def onward_z(p, j):
        block = gathered.at[row_of(behind[j]), piece_of(p)]
        return remote(block, block, out_send, out_recv.at[slot(p) + 2], partner)

    def await_pieces(p, sem, count):
        blocks = got.at[pl.ds(0, count), piece_of(p)]
        remote(blocks, blocks, out_send, out_recv.at[slot(p) + sem], partner).wait_recv()

    def finish_piece(p):
        part = pl.ds(p * PIECE, PIECE)
        pick = picks[part, :]
        trust_block = jnp.dot(
            pick, first_terms, preferred_element_type=jnp.float32
        ) + jnp.dot(pick, last_term, preferred_element_type=jnp.float32)
        new_master = master[part, :] - learn_rate * (update[part, :] * trust_block)
        master[part, :] = new_master
        gathered[me, part, :] = new_master.astype(jnp.bfloat16)

    def forward_x(p):
        await_pieces(p, 0, 1)
        for j in range(3):
            onward_x(p, j).start()

    def forward_z(p):
        await_pieces(p, 0, 2)
        onward_z(p, 0).start()
        onward_z(p, 1).start()
        await_pieces(p, 1, 1)
        onward_z(p, 2).start()

    def collect(p):
        if p in Z_FIRST:
            await_pieces(p, 2, 5)
        else:
            await_pieces(p, 2, 4)
        for r in range(REPLICAS):
            spread[pl.ds(r, PIECE, stride=8), :] = gathered[r, piece_of(p), :].astype(jnp.float32)

        def tile(t, carry):
            for i in range(8):
                at = t * 8 + i
                cols = pl.ds(pl.multiple_of((p * PIECE + at) * LANES, LANES), LANES)
                packed[:, cols] = spread[pl.ds(pl.multiple_of(at * 8, 8), 8), :].astype(
                    jnp.bfloat16
                )
            return carry

        lax.fori_loop(0, PIECE // 8, tile, 0)

    for p in range(PIECES):
        finish_piece(p)
        if p in Z_FIRST:
            direct(p, 0).start()
        else:
            for i in range(1, 4):
                direct(p, i).start()
    for p in Z_FIRST:
        direct(p, 1).start()
        direct(p, 2).start()
    for p in X_FIRST:
        direct(p, 0).start()
    for k in range(max(len(Z_FIRST), len(X_FIRST))):
        if k < len(X_FIRST):
            forward_z(X_FIRST[k])
        if k < len(Z_FIRST):
            forward_x(Z_FIRST[k])
    for p in Z_FIRST:
        await_pieces(p, 1, 1)
        relay(p).start()
    for p in X_FIRST + Z_FIRST:
        collect(p)

    shared = rows.at[:, pl.ds(0, len(SUMMED) * CHUNK)]
    remote(shared, shared, send_sem.at[0], recv_sem.at[0], partner).wait_send()
    for c in range(CHUNKS):
        if c not in SUMMED:
            straight = got.at[:, part_of(c)]
            remote(straight, straight, send_sem.at[1], recv_sem.at[c], partner).wait_send()
    remote(theirs, theirs, sum_send, sum_recv, partner).wait_send()
    remote(got, got, out_send, out_recv.at[0], partner).wait_send()


def hand_over(*refs):
    sem = refs[-1]
    copies = [pltpu.make_async_copy(refs[i], refs[4 + i], sem.at[i]) for i in range(4)]
    for copy in copies:
        copy.start()
    for copy in copies:
        copy.wait()


def on_device(gradients, master, moment, second, segment_ids):
    flat = master.shape[0]
    tall = (BLOCKS, LANES)
    f32, bf16 = jnp.float32, jnp.bfloat16
    vmem_spec = pl.BlockSpec(memory_space=pltpu.VMEM)
    dma = pltpu.SemaphoreType.DMA
    weights, new_master, new_moment, new_second = pl.pallas_call(
        kernel,
        out_shape=(
            jax.ShapeDtypeStruct((REPLICAS, flat), bf16),
            jax.ShapeDtypeStruct(tall, f32),
            jax.ShapeDtypeStruct(tall, f32),
            jax.ShapeDtypeStruct(tall, f32),
        ),
        in_specs=[pl.BlockSpec(memory_space=pltpu.HBM)] * 5,
        out_specs=(vmem_spec,) * 4,
        scratch_shapes=[
            pltpu.VMEM((REPLICAS, flat), bf16),
            pltpu.VMEM((REPLICAS, BLOCKS, LANES), bf16),
            pltpu.VMEM((len(STEPS), BLOCKS, LANES), bf16),
            pltpu.VMEM(tall, f32),
            pltpu.VMEM(tall, f32),
            pltpu.VMEM(tall, f32),
            pltpu.VMEM((CHUNKS, CHUNK), jnp.int32),
            pltpu.VMEM((BLOCKS, LANES), bf16),
            pltpu.VMEM((CHUNK, LANES), f32),
            pltpu.VMEM((2 * TENSORS, LANES), f32),
            pltpu.VMEM((8, LANES), f32),
            pltpu.VMEM((len(OFFSETS), LANES), f32),
            pltpu.VMEM((CHUNK * 8, LANES), f32),
            pltpu.VMEM((REPLICAS, BLOCKS, LANES), bf16),
            dma((CHUNKS,)),
            dma((4,)),
            dma((2,)),
            dma((CHUNKS + len(SUMMED),)),
            dma,
            dma,
            dma,
            dma((PIECES * 3,)),
        ],
        compiler_params=pltpu.CompilerParams(
            collective_id=0, has_side_effects=True, vmem_limit_bytes=40 << 20
        ),
        name="lamb_step",
    )(
        *(
            pltpu.with_memory_space_constraint(array, pltpu.HBM)
            for array in (
                gradients.reshape(REPLICAS, flat),
                master.reshape(tall),
                moment.reshape(tall),
                second.reshape(tall),
                segment_ids.reshape(CHUNKS, CHUNK),
            )
        )
    )
    weights, new_master, new_moment, new_second = pl.pallas_call(
        hand_over,
        out_shape=(
            jax.ShapeDtypeStruct((REPLICAS, flat), bf16),
            jax.ShapeDtypeStruct(tall, f32),
            jax.ShapeDtypeStruct(tall, f32),
            jax.ShapeDtypeStruct(tall, f32),
        ),
        in_specs=[vmem_spec] * 4,
        out_specs=(pl.BlockSpec(memory_space=pltpu.HBM),) * 4,
        scratch_shapes=[dma((4,))],
        compiler_params=pltpu.CompilerParams(vmem_limit_bytes=8 << 20),
        name="hand_over",
    )(weights, new_master, new_moment, new_second)
    return (weights, new_master.reshape(-1), new_moment.reshape(-1), new_second.reshape(-1))


def solution(mesh):
    torus = Mesh(mesh.devices.reshape(2, 4, 4, 2, 2), AXES)
    return jax.shard_map(
        on_device,
        mesh=torus,
        in_specs=(P(DP, None, SHARD), P(DP_SHARD), P(DP_SHARD), P(DP_SHARD), P(DP_SHARD)),
        out_specs=(P(None, SHARD), P(DP_SHARD), P(DP_SHARD), P(DP_SHARD)),
        check_vma=False,
    )
```

```python
import functools

import jax
import jax.numpy as jnp
from jax import lax
from jax.experimental import pallas as pl
from jax.experimental.pallas import tpu as pltpu
from jax.sharding import Mesh
from jax.sharding import PartitionSpec as P

AXES = ("zh", "x", "y", "zl", "core")
DP = ("zh", "x")
SHARD = ("y", "zl", "core")
DP_SHARD = AXES
MESH = pl.DeviceIdType.MESH

first_fix = 1.0 - 0.9**20
second_fix = 1.0 - 0.999**20
learn_rate = 0.2
decay_rate = 0.01
tiny_eps = 1e-06

REPLICAS = 8
TENSORS = 64
BLOCKS = 768
LANES = 128
CHUNK = 128
CHUNKS = BLOCKS // CHUNK
SUB = 32
PIECE = 128
PIECES = BLOCKS // PIECE
REACH = 4
Z_FIRST = (1, 3, 5)
X_FIRST = tuple(p for p in range(PIECES) if p not in Z_FIRST)
LAG = 4
HIGH = lax.Precision.HIGHEST

STEPS = ((1, 1), (3, 0), (2, 1), (1, 0), (0, 1), (3, 1), (2, 0))
X_STEPS = (1, 3, 2)
ROUTES = ("plane", "plane", 1, 3, "direct", "direct")
SUMMED = tuple(c for c in range(CHUNKS) if ROUTES[c] != "direct")
OFFSETS = tuple(range(-REACH, 0)) + tuple(range(1, REACH + 1))


def place():
    return {axis: lax.axis_index(axis) for axis in AXES}


def replica_at(here, x_step, z_step):
    there = dict(here)
    there["x"] = lax.rem(here["x"] + x_step, 4)
    there["zh"] = lax.rem(here["zh"] + z_step, 2)
    return there


def row_of(there):
    return there["zh"] * 4 + there["x"]


def flat_neighbour(here, offset):
    rank = (((here["zh"] * 4 + here["x"]) * 4 + here["y"]) * 2 + here["zl"]) * 2 + here["core"]
    rank = lax.rem(rank + offset + 128, 128)
    return {
        "zh": rank // 64,
        "x": lax.rem(rank // 16, 4),
        "y": lax.rem(rank // 4, 4),
        "zl": lax.rem(rank // 2, 2),
        "core": lax.rem(rank, 2),
    }


def remote(src, dst, send_sem, recv_sem, there):
    return pltpu.make_async_remote_copy(
        src_ref=src,
        dst_ref=dst,
        send_sem=send_sem,
        recv_sem=recv_sem,
        device_id=there,
        device_id_type=MESH,
    )


def kernel(
    grad_hbm, master_hbm, moment_hbm, second_hbm, ids_hbm,
    packed, master, moment, second,
    grad_in, rows, got, sum_out, sum_in, update, ids, picks, squares, sums,
    mine, theirs, spread, gathered,
    load_sem, state_sem, send_sem, recv_sem, sum_send, sum_recv,
    out_send, out_recv,
):
    here = place()
    me = row_of(here)
    peers = [replica_at(here, a, b) for a, b in STEPS]
    neighbours = [flat_neighbour(here, k) for k in OFFSETS]

    barrier = pltpu.get_barrier_semaphore()
    for there in peers + neighbours:
        pl.semaphore_signal(barrier, inc=1, device_id=there, device_id_type=MESH)

    def load(c):
        cols = pl.ds(pl.multiple_of(c * CHUNK * LANES, CHUNK * LANES), CHUNK * LANES)
        return pltpu.make_async_copy(grad_hbm.at[:, cols], grad_in.at[:, cols], load_sem.at[c])

    for c in range(CHUNKS):
        load(c).start()
    state_loads = [
        pltpu.make_async_copy(src, dst, state_sem.at[i])
        for i, (src, dst) in enumerate(
            ((ids_hbm, ids), (master_hbm, master), (moment_hbm, moment), (second_hbm, second))
        )
    ]
    for copy in state_loads:
        copy.start()

    def split_rows(c):
        load(c).wait()

        def tile(t, carry):
            at = c * CHUNK + t * 8
            for i in range(8):
                cols = pl.ds(pl.multiple_of((at + i) * LANES, LANES), LANES)
                spread[pl.ds(pl.multiple_of((t * 8 + i) * 8, 8), 8), :] = grad_in[:, cols].astype(
                    jnp.float32
                )
            return carry

        lax.fori_loop(0, CHUNK // 8, tile, 0)
        for r in range(REPLICAS):
            for h in range(CHUNK // SUB):
                piece = spread[pl.ds(h * SUB * 8 + r, SUB, stride=8), :]
                rows[r, pl.ds(pl.multiple_of(c * CHUNK + h * SUB, SUB), SUB), :] = piece.astype(
                    jnp.bfloat16
                )

    def part_of(c):
        return pl.ds(c * CHUNK, CHUNK)

    partner = replica_at(here, 0, 1)

    def sends(c):
        route = ROUTES[c]
        if route == "direct":
            return [(there, there, k) for k, there in enumerate(peers)]
        if route == "plane":
            out = []
            for j, a in enumerate(X_STEPS):
                there = replica_at(here, a, 0)
                out.append((replica_at(here, a, 1), there, 3 + j))
                out.append((there, there, j))
            return out
        near, back = route, 4 - route
        return [
            (replica_at(here, 2, 1), replica_at(here, back, 1), 4),
            (replica_at(here, 2, 0), replica_at(here, back, 0), 3),
            (replica_at(here, back, 1), partner, 5),
            (replica_at(here, near, 1), replica_at(here, near, 1), 1),
            (partner, partner, 2),
            (replica_at(here, near, 0), replica_at(here, near, 0), 0),
        ]

    def sum_target(c):
        return partner if ROUTES[c] == "plane" else replica_at(here, 4 - ROUTES[c], 0)

    def send_rows(c):
        for owner, there, at in sends(c):
            direct_route = ROUTES[c] == "direct"
            remote(
                rows.at[row_of(owner), part_of(c)], got.at[at, part_of(c)],
                send_sem.at[1 if direct_route else 0],
                recv_sem.at[CHUNKS + SUMMED.index(c) if at >= 3 and not direct_route else c], there,
            ).start()

    def await_rows(c, stage, first, count):
        part = got.at[pl.ds(first, count), part_of(c)]
        remote(part, part, send_sem.at[0], recv_sem.at[CHUNKS + SUMMED.index(c) if stage else c], partner).wait_recv()

    def send_sum(c):
        await_rows(c, 1, 3, 3)
        there = sum_target(c)
        owner = row_of(there)

        def add(h, carry):
            part = pl.ds(pl.multiple_of(c * CHUNK + h * SUB, SUB), SUB)
            total = rows[owner, part, :].astype(jnp.float32)
            for k in range(3, 6):
                total = total + got[k, part, :].astype(jnp.float32)
            sum_out[part, :] = total
            return carry

        lax.fori_loop(0, CHUNK // SUB, add, 0)
        remote(
            sum_out.at[part_of(c)], sum_in.at[part_of(c)],
            send_sem.at[0], recv_sem.at[c], there,
        ).start()

    for c in range(CHUNKS):
        split_rows(c)
        if c == 0:
            pl.semaphore_wait(barrier, len(peers) + len(neighbours))
        send_rows(c)

    for copy in state_loads:
        copy.wait()

    def onehot(c):
        tensor = lax.broadcasted_iota(jnp.int32, (TENSORS, CHUNK), 0)
        return (tensor == ids[pl.ds(c, 1), :]).astype(jnp.float32)

    sums[...] = jnp.zeros_like(sums)
    wide = lax.broadcasted_iota(jnp.int32, (2 * TENSORS, LANES), 0)
    lane = lax.broadcasted_iota(jnp.int32, (2 * TENSORS, LANES), 1)
    upper = wide < TENSORS
    tensor_of = jnp.where(upper, wide, wide - TENSORS)

    def index_blocks(c, carry):
        chosen = (tensor_of == ids[pl.ds(c, 1), :]).astype(jnp.float32)
        picks[pl.ds(pl.multiple_of(c * CHUNK, CHUNK), CHUNK), :] = chosen.T.astype(jnp.bfloat16)
        return carry

    lax.fori_loop(0, CHUNKS, index_blocks, 0)

    def weigh(c, carry):
        values = master[pl.ds(pl.multiple_of(c * CHUNK, CHUNK), CHUNK), :]
        sums[:TENSORS, :] += jnp.dot(
            onehot(c), values * values, precision=HIGH, preferred_element_type=jnp.float32
        )
        return carry

    lax.fori_loop(0, CHUNKS, weigh, 0)

    def step_chunk(c):
        direct_route = ROUTES[c] == "direct"
        await_rows(c, 0, 0, 7 if direct_route else 5)

        def step(h, carry):
            part = pl.ds(pl.multiple_of(c * CHUNK + h * SUB, SUB), SUB)
            total = rows[me, part, :].astype(jnp.float32)
            for k in range(7 if direct_route else 3):
                total = total + got[k, part, :].astype(jnp.float32)
            if not direct_route:
                total = total + sum_in[part, :]
            grad = total / REPLICAS
            next_moment = 0.9 * moment[part, :] + 0.1 * grad
            next_second = 0.999 * second[part, :] + 0.001 * grad * grad
            change = (
                next_moment / first_fix / (jnp.sqrt(next_second / second_fix) + tiny_eps)
                + decay_rate * master[part, :]
            )
            moment[part, :] = next_moment
            second[part, :] = next_second
            update[part, :] = change
            squares[pl.ds(pl.multiple_of(h * SUB, SUB), SUB), :] = change * change
            return carry

        lax.fori_loop(0, CHUNK // SUB, step, 0)
        sums[TENSORS:, :] += jnp.dot(
            onehot(c), squares[...], precision=HIGH, preferred_element_type=jnp.float32
        )

    for c in range(CHUNKS + LAG):
        if c in SUMMED:
            send_sum(c)
        if c >= LAG:
            step_chunk(c - LAG)

    per_tensor = jnp.sum(sums[...], axis=1, keepdims=True)
    mine[...] = jnp.broadcast_to(
        jnp.sum(jnp.where(wide == lane, per_tensor, 0.0), axis=0, keepdims=True), (8, LANES)
    )
    swaps = [
        remote(mine.at[pl.ds(0, 1)], theirs.at[pl.ds(i, 1)], sum_send, sum_recv, neighbours[len(OFFSETS) - 1 - i])
        for i in range(len(OFFSETS))
    ]
    for copy in swaps:
        copy.start()
    all_swaps = remote(theirs, theirs, sum_send, sum_recv, neighbours[0])
    all_swaps.wait_recv()
    total = mine[...] + jnp.sum(theirs[...], axis=0, keepdims=True)
    trust = jnp.sqrt(total) / (jnp.sqrt(pltpu.roll(total, TENSORS, 1)) + tiny_eps)
    trust_row = trust[:1, :]
    trust_of = jnp.sum(jnp.where(tensor_of == lane, trust_row, 0.0), axis=1, keepdims=True)
    trust_of = jnp.broadcast_to(trust_of, (2 * TENSORS, LANES))
    high = trust_of.astype(jnp.bfloat16).astype(jnp.float32)
    middle = (trust_of - high).astype(jnp.bfloat16).astype(jnp.float32)
    low = trust_of - high - middle
    first_terms = jnp.where(upper, high, middle).astype(jnp.bfloat16)
    last_term = jnp.where(upper, low, 0.0).astype(jnp.bfloat16)

    beside = [replica_at(here, a, 0) for a in X_STEPS]
    behind = [replica_at(here, 4 - a, 0) for a in X_STEPS]
    direct_to = [partner] + beside

    def piece_of(p):
        return pl.ds(pl.multiple_of(p * PIECE, PIECE), PIECE)

    def slot(p):
        return 3 * p

    def direct(p, i):
        block = gathered.at[me, piece_of(p)]
        if p in Z_FIRST:
            sem = (0, 1 + Z_FIRST.index(p) % 2, 2 - Z_FIRST.index(p) % 2)[i]
        else:
            sem = (2, 0, 0, 1)[i]
        return remote(block, block, out_send, out_recv.at[slot(p) + sem], direct_to[i])

    def relay(p):
        turn = Z_FIRST.index(p) % 2
        block = gathered.at[row_of(behind[turn]), piece_of(p)]
        return remote(block, block, out_send, out_recv.at[slot(p) + 2], beside[turn])

    def onward_x(p, j):
        block = gathered.at[row_of(partner), piece_of(p)]
        return remote(block, block, out_send, out_recv.at[slot(p) + 2], beside[j])

    def onward_z(p, j):
        block = gathered.at[row_of(behind[j]), piece_of(p)]
        return remote(block, block, out_send, out_recv.at[slot(p) + 2], partner)

    def await_pieces(p, sem, count):
        blocks = got.at[pl.ds(0, count), piece_of(p)]
        remote(blocks, blocks, out_send, out_recv.at[slot(p) + sem], partner).wait_recv()

    def finish_piece(p):
        part = pl.ds(p * PIECE, PIECE)
        pick = picks[part, :]
        trust_block = jnp.dot(
            pick, first_terms, preferred_element_type=jnp.float32
        ) + jnp.dot(pick, last_term, preferred_element_type=jnp.float32)
        new_master = master[part, :] - learn_rate * (update[part, :] * trust_block)
        master[part, :] = new_master
        gathered[me, part, :] = new_master.astype(jnp.bfloat16)

    def forward_x(p):
        await_pieces(p, 0, 1)
        for j in range(3):
            onward_x(p, j).start()

    def forward_z(p):
        await_pieces(p, 0, 2)
        onward_z(p, 0).start()
        onward_z(p, 1).start()
        await_pieces(p, 1, 1)
        onward_z(p, 2).start()

    def collect(p):
        if p in Z_FIRST:
            await_pieces(p, 2, 5)
        else:
            await_pieces(p, 2, 4)
        for r in range(REPLICAS):
            spread[pl.ds(r, PIECE, stride=8), :] = gathered[r, piece_of(p), :].astype(jnp.float32)

        def tile(t, carry):
            for i in range(8):
                at = t * 8 + i
                cols = pl.ds(pl.multiple_of((p * PIECE + at) * LANES, LANES), LANES)
                packed[:, cols] = spread[pl.ds(pl.multiple_of(at * 8, 8), 8), :].astype(
                    jnp.bfloat16
                )
            return carry

        lax.fori_loop(0, PIECE // 8, tile, 0)

    for p in range(PIECES):
        finish_piece(p)
        if p in Z_FIRST:
            direct(p, 0).start()
        else:
            for i in range(1, 4):
                direct(p, i).start()
    for p in Z_FIRST:
        direct(p, 1).start()
        direct(p, 2).start()
    for p in X_FIRST:
        direct(p, 0).start()
    for k in range(max(len(Z_FIRST), len(X_FIRST))):
        if k < len(X_FIRST):
            forward_z(X_FIRST[k])
        if k < len(Z_FIRST):
            forward_x(Z_FIRST[k])
    for p in Z_FIRST:
        await_pieces(p, 1, 1)
        relay(p).start()
    for p in X_FIRST + Z_FIRST:
        collect(p)

    shared = rows.at[:, pl.ds(0, len(SUMMED) * CHUNK)]
    remote(shared, shared, send_sem.at[0], recv_sem.at[0], partner).wait_send()
    for c in range(CHUNKS):
        if c not in SUMMED:
            straight = got.at[:, part_of(c)]
            remote(straight, straight, send_sem.at[1], recv_sem.at[c], partner).wait_send()
    remote(theirs, theirs, sum_send, sum_recv, partner).wait_send()
    remote(got, got, out_send, out_recv.at[0], partner).wait_send()


def hand_over(*refs):
    sem = refs[-1]
    copies = [pltpu.make_async_copy(refs[i], refs[4 + i], sem.at[i]) for i in range(4)]
    for copy in copies:
        copy.start()
    for copy in copies:
        copy.wait()


def on_device(gradients, master, moment, second, segment_ids):
    flat = master.shape[0]
    tall = (BLOCKS, LANES)
    f32, bf16 = jnp.float32, jnp.bfloat16
    vmem_spec = pl.BlockSpec(memory_space=pltpu.VMEM)
    dma = pltpu.SemaphoreType.DMA
    weights, new_master, new_moment, new_second = pl.pallas_call(
        kernel,
        out_shape=(
            jax.ShapeDtypeStruct((REPLICAS, flat), bf16),
            jax.ShapeDtypeStruct(tall, f32),
            jax.ShapeDtypeStruct(tall, f32),
            jax.ShapeDtypeStruct(tall, f32),
        ),
        in_specs=[pl.BlockSpec(memory_space=pltpu.HBM)] * 5,
        out_specs=(vmem_spec,) * 4,
        scratch_shapes=[
            pltpu.VMEM((REPLICAS, flat), bf16),
            pltpu.VMEM((REPLICAS, BLOCKS, LANES), bf16),
            pltpu.VMEM((len(STEPS), BLOCKS, LANES), bf16),
            pltpu.VMEM(tall, f32),
            pltpu.VMEM(tall, f32),
            pltpu.VMEM(tall, f32),
            pltpu.VMEM((CHUNKS, CHUNK), jnp.int32),
            pltpu.VMEM((BLOCKS, LANES), bf16),
            pltpu.VMEM((CHUNK, LANES), f32),
            pltpu.VMEM((2 * TENSORS, LANES), f32),
            pltpu.VMEM((8, LANES), f32),
            pltpu.VMEM((len(OFFSETS), LANES), f32),
            pltpu.VMEM((CHUNK * 8, LANES), f32),
            pltpu.VMEM((REPLICAS, BLOCKS, LANES), bf16),
            dma((CHUNKS,)),
            dma((4,)),
            dma((2,)),
            dma((CHUNKS + len(SUMMED),)),
            dma,
            dma,
            dma,
            dma((PIECES * 3,)),
        ],
        compiler_params=pltpu.CompilerParams(
            collective_id=0, has_side_effects=True, vmem_limit_bytes=40 << 20
        ),
        name="lamb_step",
    )(
        *(
            pltpu.with_memory_space_constraint(array, pltpu.HBM)
            for array in (
                gradients.reshape(REPLICAS, flat),
                master.reshape(tall),
                moment.reshape(tall),
                second.reshape(tall),
                segment_ids.reshape(CHUNKS, CHUNK),
            )
        )
    )
    weights, new_master, new_moment, new_second = pl.pallas_call(
        hand_over,
        out_shape=(
            jax.ShapeDtypeStruct((REPLICAS, flat), bf16),
            jax.ShapeDtypeStruct(tall, f32),
            jax.ShapeDtypeStruct(tall, f32),
            jax.ShapeDtypeStruct(tall, f32),
        ),
        in_specs=[vmem_spec] * 4,
        out_specs=(pl.BlockSpec(memory_space=pltpu.HBM),) * 4,
        scratch_shapes=[dma((4,))],
        compiler_params=pltpu.CompilerParams(vmem_limit_bytes=8 << 20),
        name="hand_over",
    )(weights, new_master, new_moment, new_second)
    return (weights, new_master.reshape(-1), new_moment.reshape(-1), new_second.reshape(-1))


def solution(mesh):
    torus = Mesh(mesh.devices.reshape(2, 4, 4, 2, 2), AXES)
    return jax.shard_map(
        on_device,
        mesh=torus,
        in_specs=(P(DP, None, SHARD), P(DP_SHARD), P(DP_SHARD), P(DP_SHARD), P(DP_SHARD)),
        out_specs=(P(None, SHARD), P(DP_SHARD), P(DP_SHARD), P(DP_SHARD)),
        check_vma=False,
    )
```
